256 devices in a mesh: rows: 32 (over z, y), cls: 8 (over x, core).
Axes of the slice: x: 4, y: 4, z: 8, core: 2. Of those that a mesh axis runs over, the one named last changes fastest.
Arguments:
- embeddings: bfloat16 [65536, 1024], P('rows'), may hold values from -6 to 6
- residuals: float32 [65536, 1024], P('rows', 'cls'), may hold values from -6 to 6
- projections: bfloat16 [64, 1024, 512], P('rows'), may hold values from -0.1875 to 0.1875
- phases: bfloat16 [64, 512], P('rows'), may hold values from -3.140625 to 3.140625
- old_coef: float32 [2, 512, 1024], P(None, None, 'cls'), may hold values from -6 to 6
- block_order: int32 [2], replicated, may hold values from 0 to 63, as said below
Outputs:
- new_residuals: float32 [65536, 1024], P('rows', 'cls')
- new_coef: float32 [2, 512, 1024], P(None, None, 'cls')
The draws below stay inside these ranges and needn't reach their ends.
Inputs may be any that keep to these rules, and one draw needn't show every extreme that they name: `block_order`: the 2 entries are distinct block numbers, one of them 64 - 1; block k is held by index k // 2 of rows.
All inputs are finite; a program needn't handle non-finite values.
Results may differ from the reference program's by a relative error of at most 0.0028.
Values may be sent and summed in bfloat16 or wider, within the bound.
No kernel may reach another device: no remote copies, remote signals or barrier semaphores. Data moves between devices by JAX's collectives and lax.ppermute only.
A program may use at most 64 MiB of HBM per device.

```python
import jax
import jax.numpy as jnp
from jax import lax

D = 1024
P_SIZE = 512
C = 1024
STEPS = 2
ROWS = 65536
NBLK = 64


def draw_block_order(key, part):
    others = jax.random.permutation(jax.random.fold_in(key, 11), NBLK - 1)[:STEPS]
    where_last = jax.random.randint(jax.random.fold_in(key, 12), (), 0, STEPS)
    places = jnp.arange(STEPS)
    order = jnp.where(places == where_last, NBLK - 1, others)
    return order.astype(jnp.int32)


def levels(stream_key, dims, cuts, smallest, high):
    gain, own = 1.0, jax.random.fold_in(stream_key, 6)
    for position, parts in cuts:
        steps = jnp.exp(jax.random.uniform(jax.random.fold_in(own, position), (parts,), jnp.float32, smallest / len(cuts), high / len(cuts)))
        gain = gain * jnp.repeat(steps, dims[position] // parts).reshape([-1 if axis == position else 1 for axis in range(len(dims))])
    return gain


def noise(stream_key, shape, deviation, reach, split=(), kind=jnp.bfloat16):
    factor_of = levels(stream_key, shape, split, -0.22, 0.18) if split else 1.0
    entries = jax.random.normal(stream_key, shape, jnp.float32) * deviation * factor_of
    return jnp.minimum(jnp.maximum(entries, -reach), reach).astype(kind)


def setup_inputs(seed: int = 0) -> dict:
    seeds = jax.random.split(jax.random.key(seed), 7)
    return {
        "embeddings": noise(seeds[0], (ROWS, D), 1.0, 6.0, ((0, 32),)),
        "residuals": noise(seeds[1], (ROWS, C), 1.0, 6.0, ((0, 32), (1, 8)), jnp.float32),
        "projections": noise(seeds[2], (NBLK, D, P_SIZE), D ** -0.5, 0.1875, ((0, 32),)),
        "phases": jnp.clip(jax.random.uniform(seeds[3], (NBLK, P_SIZE), jnp.float32, -3.140625, 3.140625), -3.140625, 3.140625).astype(jnp.bfloat16),
        "old_coef": noise(seeds[4], (STEPS, P_SIZE, C), 1.0, 6.0, ((2, 8),), jnp.float32),
        "block_order": draw_block_order(jax.random.fold_in(seeds[6], 71), 0),
    }


HIGH = lax.Precision.HIGHEST

def solve_chol(matrix, right):
    lower = jnp.linalg.cholesky(matrix)
    middle = lax.linalg.triangular_solve(lower, right, left_side=True, lower=True)
    return lax.linalg.triangular_solve(lower, middle, left_side=True, lower=True, transpose_a=True)

def reference(embeddings, residuals, projections, phases, old_coef, block_order):
    total_rows = embeddings.shape[0]
    ridge = 0.25 * total_rows / P_SIZE
    scale = 1.0 / P_SIZE ** 0.5
    current = residuals
    results = []
    for step in range(STEPS):
        block = block_order[step]
        weight = projections[block]
        shift = phases[block].astype(jnp.float32)
        angles = jnp.dot(embeddings.astype(jnp.float32), weight.astype(jnp.float32), preferred_element_type=jnp.float32) + shift
        feats = (jnp.cos(angles) * scale).astype(jnp.bfloat16)
        gram = lax.dot_general(feats.astype(jnp.float32), feats.astype(jnp.float32), (((0,), (0,)), ((), ())), preferred_element_type=jnp.float32)
        wide = feats.astype(jnp.float32)
        cross = lax.dot_general(wide, current, (((0,), (0,)), ((), ())), precision=HIGH)
        right = cross + jnp.dot(gram, old_coef[step], precision=HIGH)
        system = gram + ridge * jnp.eye(P_SIZE, dtype=jnp.float32)
        fresh = solve_chol(system, right)
        current = current - jnp.dot(wide, fresh - old_coef[step], precision=HIGH)
        results.append(fresh)
    return (current, jnp.stack(results))
```

```python
import functools
import math

import jax
import jax.numpy as jnp
from jax import lax
from jax.experimental import pallas as pl
from jax.experimental.pallas import tpu as pltpu
from jax.sharding import Mesh
from jax.sharding import PartitionSpec as P

STEPS = 2
BF = jnp.bfloat16
F32 = jnp.float32
ROWS = ("z", "y")
CLS = ("x", "c")

SINE = (
    6.283185160088491,
    -41.34165503116555,
    81.60100405640866,
    -76.54978188256763,
    39.536702776697375,
)
TOLERANCE = 1e-6
MAX_LOOPS = 2000


def cosine(angle, scale):
    turns = angle * (1.0 / (2.0 * math.pi))
    offset = turns - lax.round(turns, lax.RoundingMethod.TO_NEAREST_EVEN)
    q = 0.25 - jnp.abs(offset)
    z = q * q
    total = SINE[-1] * scale
    for coefficient in SINE[-2::-1]:
        total = total * z + coefficient * scale
    return total * q


def split_two(values):
    upper = values.astype(BF)
    return upper, (values - upper.astype(F32)).astype(BF)


def feature_kernel(place, e_ref, w_ref, shift_ref, r_ref, f_ref, out_ref, acc_ref):
    step = pl.program_id(0)
    rows = e_ref.shape[0]
    width = w_ref.shape[2]
    scale = 1.0 / width**0.5
    chunk = 256
    e = e_ref[...]
    for s in range(STEPS):
        for col in range(0, width, chunk):
            angle = jnp.dot(e, w_ref[s, :, col : col + chunk], preferred_element_type=F32)
            angle = angle + shift_ref[s : s + 1, col : col + chunk]
            f_ref[:, s * width + col : s * width + col + chunk] = cosine(angle, scale).astype(BF)
    lane = pl.multiple_of(place[0] * 128, 128)
    upper, lower = split_two(r_ref[...].T)
    left = [upper, lower]
    for s in range(STEPS):
        left.append(f_ref[:, pl.ds(pl.multiple_of(s * width + lane, 128), 128)].T)
    left = jnp.concatenate(left, axis=0)
    part = jnp.dot(left, f_ref[...], preferred_element_type=F32)

    @pl.when(step == 0)
    def _():
        acc_ref[...] = part

    @pl.when(step > 0)
    def _():
        acc_ref[...] += part

    @pl.when(step == pl.num_programs(0) - 1)
    def _():
        half = pl.multiple_of(place[1] * 256, 128)
        for group, (row, first) in enumerate(((256, 0), (384, width), (384, 0))):
            for side in range(2):
                lanes = pl.ds(pl.multiple_of(first + half + side * 128, 128), 128)
                block = acc_ref[row : row + 128, lanes]
                out_ref[side * 16 : side * 16 + 16, group * 8 : group * 8 + 8, :] = block.reshape(16, 8, 128)
        cross = acc_ref[0:128, :] + acc_ref[128:256, :]
        out_ref[:, 24:56, :] = cross.T.reshape(32, 32, 128)


def features(embeddings, weights, shifts, residuals, place):
    total, depth = embeddings.shape
    width = weights.shape[2]
    tile = 512
    return pl.pallas_call(
        feature_kernel,
        grid_spec=pltpu.PrefetchScalarGridSpec(
            num_scalar_prefetch=1,
            grid=(total // tile,),
            in_specs=[
                pl.BlockSpec((tile, depth), lambda i, p: (i, 0)),
                pl.BlockSpec((STEPS, depth, width), lambda i, p: (0, 0, 0)),
                pl.BlockSpec((STEPS, width), lambda i, p: (0, 0)),
                pl.BlockSpec((tile, 128), lambda i, p: (i, 0)),
            ],
            out_specs=[
                pl.BlockSpec((tile, STEPS * width), lambda i, p: (i, 0)),
                pl.BlockSpec((32, 56, 128), lambda i, p: (0, 0, 0)),
            ],
            scratch_shapes=[pltpu.VMEM((512, STEPS * width), F32)],
        ),
        out_shape=[
            jax.ShapeDtypeStruct((total, STEPS * width), BF),
            jax.ShapeDtypeStruct((32, 56, 128), F32),
        ],
        compiler_params=pltpu.CompilerParams(vmem_limit_bytes=40 << 20),
        name="features",
    )(place, embeddings, weights, shifts, residuals)


def times(upper, lower, values):
    high, low = split_two(values)
    both = jnp.dot(upper, jnp.concatenate([high, low], axis=1), preferred_element_type=F32)
    return both[:, :128] + both[:, 128:] + jnp.dot(lower, high, preferred_element_type=F32)


def conjugate_gradients(upper_ref, lower_ref, right, ridge):
    size = jnp.sum(right * right, axis=0, keepdims=True)
    floor = size * (TOLERANCE * TOLERANCE)

    def one(x, r, p, rr):
        ap = times(upper_ref[...], lower_ref[...], p) + ridge * p
        curve = jnp.sum(p * ap, axis=0, keepdims=True)
        alpha = jnp.where(curve > 0.0, rr / curve, 0.0)
        x = x + alpha * p
        r = r - alpha * ap
        new = jnp.sum(r * r, axis=0, keepdims=True)
        beta = jnp.where(rr > 0.0, new / rr, 0.0)
        return x, r, r + beta * p, new

    def body(state):
        count, x, r, p, rr = state
        for _ in range(2):
            x, r, p, rr = one(x, r, p, rr)
        return count + 1, x, r, p, rr

    def open_still(state):
        return jnp.logical_and(state[0] < MAX_LOOPS, jnp.max(state[4] - floor) > 0.0)

    state = (jnp.int32(0), jnp.zeros_like(right), right, right, size)
    return lax.while_loop(open_still, body, state)[1]


def solve_kernel(ridge, place, *refs):
    pieces = refs[:8]
    all_ref, old_ref, f_ref, r_ref, coef_ref, out_ref, upper, lower = refs[8:]
    for shift in range(4):
        for other in range(2):
            ref = pieces[shift * 2 + other]
            px = lax.rem(place[0] + 4 - shift, 4)
            pc = lax.rem(place[1] + other, 2)
            row = pl.multiple_of(px * 128, 128)
            for group in range(3):
                for side in range(2):
                    lanes = pl.ds(pl.multiple_of(pc * 256 + side * 128, 128), 128)
                    block = ref[side * 16 : side * 16 + 16, group * 8 : group * 8 + 8, :].reshape(128, 128)
                    high, low = split_two(block)
                    upper[group, pl.ds(row, 128), lanes] = high
                    lower[group, pl.ds(row, 128), lanes] = low
    cross = all_ref[:, 24:56, :].reshape(1024, 128)
    first = conjugate_gradients(upper.at[0], lower.at[0], cross[:512] - ridge * old_ref[0], ridge)
    coef_ref[0] = old_ref[0] + first
    cross = cross[512:] - times(upper[2], lower[2], first)
    second = conjugate_gradients(upper.at[1], lower.at[1], cross - ridge * old_ref[1], ridge)
    coef_ref[1] = old_ref[1] + second
    high, low = split_two(jnp.concatenate([first, second], axis=0))
    delta = jnp.concatenate([high, low], axis=1)
    tile = 256
    for row in range(0, f_ref.shape[0], tile):
        both = jnp.dot(f_ref[row : row + tile, :], delta, preferred_element_type=F32)
        out_ref[row : row + tile, :] = r_ref[row : row + tile, :] - both[:, :128] - both[:, 128:]


def solve(pieces, everything, old, feats, residuals, place, ridge):
    whole = pl.BlockSpec(memory_space=pltpu.VMEM)
    return pl.pallas_call(
        functools.partial(solve_kernel, ridge),
        in_specs=[pl.BlockSpec(memory_space=pltpu.SMEM)] + [whole] * 12,
        out_specs=[whole, whole],
        out_shape=[
            jax.ShapeDtypeStruct(old.shape, F32),
            jax.ShapeDtypeStruct(residuals.shape, F32),
        ],
        scratch_shapes=[pltpu.VMEM((3, 512, 512), BF), pltpu.VMEM((3, 512, 512), BF)],
        compiler_params=pltpu.CompilerParams(vmem_limit_bytes=48 << 20),
        name="solve",
    )(place, *pieces, everything, old, feats, residuals)


def exchange(values, axes):
    return lax.all_to_all(values, axes, split_axis=0, concat_axis=0, tiled=True)


def gather(values, axes, count):
    return exchange(jnp.broadcast_to(values[None], (count,) + values.shape), axes)


def body(embeddings, residuals, projections, phases, old_coef, block_order):
    local_blocks, depth, width = projections.shape
    nx, nc = lax.axis_size("x"), lax.axis_size("c")
    nrows = lax.axis_size("z") * lax.axis_size("y")
    ix, ic = lax.axis_index("x"), lax.axis_index("c")
    ridge = 0.25 * (embeddings.shape[0] * nrows) / width
    holder = block_order // local_blocks
    slot = block_order % local_blocks
    part = depth // (nx * nc)
    at = (ix * nc + ic) * part
    share = nrows // STEPS

    sent = []
    both = jnp.concatenate([lax.dynamic_slice(phases, (slot[s], 0), (1, width)) for s in range(STEPS)], axis=0)
    both = jnp.pad(both, ((0, 8 - STEPS), (0, 0)))
    for s in range(STEPS):
        mine = lax.dynamic_slice(projections, (slot[s], at, 0), (1, part, width))
        sent.append(mine.reshape(share, part // share, width))
    sent = jnp.concatenate(sent, axis=0)
    sent = jnp.concatenate([sent, jnp.broadcast_to(both[None], (nrows, 8, width))], axis=1)
    got = exchange(sent, ROWS)
    source = holder[lax.axis_index(ROWS) // share]
    piece = lax.dynamic_slice(got, (source, 0, 0), (1, 8, width))[0]
    shifts = jnp.concatenate(
        [lax.dynamic_slice(got, (holder[s], 8 + s, 0), (1, 1, width))[0] for s in range(STEPS)], axis=0
    ).astype(F32)
    mine = gather(piece, ROWS, nrows).reshape(STEPS, part, width)
    chips = gather(mine, "x", nx)
    swap = [(i, (i + 1) % nc) for i in range(nc)]
    other = lax.ppermute(chips, "c", swap)
    even = jnp.where(ic == 0, chips, other)
    odd = jnp.where(ic == 0, other, chips)
    weights = jnp.stack([even, odd], axis=1)
    weights = weights.transpose(2, 0, 1, 3, 4).reshape(STEPS, depth, width)

    place = jnp.stack([ix, ic]).astype(jnp.int32)
    feats, parts = features(embeddings, weights, shifts, residuals, place)

    summed = jnp.sum(exchange(parts, ROWS), axis=0)
    everything = gather(summed, ROWS, nrows)
    grams = everything[:, :24, :]
    pieces = []
    for shift in range(nx):
        moved = grams
        if shift:
            moved = lax.ppermute(grams, "x", [(i, (i + shift) % nx) for i in range(nx)])
        pieces += [moved, lax.ppermute(moved, "c", swap)]
    coef, current = solve(pieces, everything, old_coef, feats, residuals, place, ridge)
    return current, coef


def solution(mesh):
    grid = Mesh(mesh.devices.reshape(8, 4, 4, 2), ROWS + CLS)
    in_specs = (
        P(ROWS, None),
        P(ROWS, CLS),
        P(ROWS, None, None),
        P(ROWS, None),
        P(None, None, CLS),
        P(),
    )
    out_specs = (P(ROWS, CLS), P(None, None, CLS))
    return jax.shard_map(body, mesh=grid, in_specs=in_specs, out_specs=out_specs, check_vma=False)
```

```python
import functools
import math

import jax
import jax.numpy as jnp
from jax import lax
from jax.experimental import pallas as pl
from jax.experimental.pallas import tpu as pltpu
from jax.sharding import Mesh
from jax.sharding import PartitionSpec as P

STEPS = 2
BF = jnp.bfloat16
F32 = jnp.float32
ROWS = ("z", "y")
CLS = ("x", "c")

SINE = (
    6.283185160088491,
    -41.34165503116555,
    81.60100405640866,
    -76.54978188256763,
    39.536702776697375,
)
TOLERANCE = 1e-6
MAX_LOOPS = 2000


def cosine(angle, scale):
    turns = angle * (1.0 / (2.0 * math.pi))
    offset = turns - lax.round(turns, lax.RoundingMethod.TO_NEAREST_EVEN)
    q = 0.25 - jnp.abs(offset)
    z = q * q
    total = SINE[-1] * scale
    for coefficient in SINE[-2::-1]:
        total = total * z + coefficient * scale
    return total * q


def split_two(values):
    upper = values.astype(BF)
    return upper, (values - upper.astype(F32)).astype(BF)


def offsets(shift, other):
    return lax.rem(lax.axis_index("x") + 4 - shift, 4), lax.rem(lax.axis_index("c") + other, 2)


def payload_kernel(local_blocks, order, proj_ref, phase_ref, out_ref):
    part = 128
    width = proj_ref.shape[2]
    share = out_ref.shape[0] // STEPS
    at = pl.multiple_of((lax.axis_index("x") * 2 + lax.axis_index("c")) * part, part)
    for s in range(STEPS):
        slot = lax.rem(order[s], local_blocks)
        mine = proj_ref[pl.ds(slot, 1), pl.ds(at, part), :]
        out_ref[s * share : (s + 1) * share, :, :width] = mine.reshape(share, part // share, width)
    bands = []
    for s in range(STEPS):
        slot = lax.rem(order[s], local_blocks)
        shift = phase_ref[0:1, :].astype(F32)
        for k in range(1, phase_ref.shape[0]):
            shift = jnp.where(slot == k, phase_ref[k : k + 1, :].astype(F32), shift)
        bands += [shift[:, q * 128 : (q + 1) * 128] for q in range(width // 128)]
    band = jnp.concatenate(bands, axis=0).astype(BF)
    out_ref[:, :, width:] = jnp.broadcast_to(band[None], (out_ref.shape[0],) + band.shape)


def payload(order, projections, phases, nrows):
    local_blocks, depth, width = projections.shape
    whole = pl.BlockSpec(memory_space=pltpu.VMEM)
    return pl.pallas_call(
        functools.partial(payload_kernel, local_blocks),
        in_specs=[pl.BlockSpec(memory_space=pltpu.SMEM), whole, whole],
        out_specs=whole,
        out_shape=jax.ShapeDtypeStruct((nrows, 8, width + 128), BF),
        name="payload",
    )(order, projections, phases)


def pick_kernel(local_blocks, order, got_ref, piece_ref, shift_ref):
    nrows, _, width = piece_ref.shape
    row = lax.axis_index("z") * 4 + lax.axis_index("y")
    source = jnp.where(row < nrows // STEPS, order[0], order[1]) // local_blocks
    piece = got_ref[pl.ds(source, 1), :, :width]
    piece_ref[...] = jnp.broadcast_to(piece, piece_ref.shape)
    for s in range(STEPS):
        band = got_ref[pl.ds(order[s] // local_blocks, 1), :, width:][0].astype(F32)
        for q in range(width // 128):
            row = s * (width // 128) + q
            shift_ref[s : s + 1, q * 128 : (q + 1) * 128] = band[row : row + 1, :]


def pick(order, got, local_blocks):
    nrows, eight, wide = got.shape
    width = wide - 128
    whole = pl.BlockSpec(memory_space=pltpu.VMEM)
    return pl.pallas_call(
        functools.partial(pick_kernel, local_blocks),
        in_specs=[pl.BlockSpec(memory_space=pltpu.SMEM), whole],
        out_specs=[whole, whole],
        out_shape=[
            jax.ShapeDtypeStruct((nrows, eight, width), BF),
            jax.ShapeDtypeStruct((STEPS, width), F32),
        ],
        name="pick",
    )(order, got)


def feature_kernel(*refs):
    pieces = refs[:8]
    e_ref, shift_ref, r_ref, f_ref, out_ref, w_ref, acc_ref = refs[8:]
    step = pl.program_id(0)
    width = w_ref.shape[2]
    scale = 1.0 / width**0.5
    chunk = 256

    @pl.when(step == 0)
    def _():
        for shift in range(4):
            for other in range(2):
                px, pc = offsets(shift, other)
                at = pl.multiple_of(px * 256 + pc * 128, 128)
                for s in range(STEPS):
                    part = pieces[shift * 2 + other][s * 16 : s * 16 + 16, :, :]
                    w_ref[s, pl.ds(at, 128), :] = part.reshape(128, width)

    e = e_ref[...]
    for s in range(STEPS):
        for col in range(0, width, chunk):
            angle = jnp.dot(e, w_ref[s, :, col : col + chunk], preferred_element_type=F32)
            angle = angle + shift_ref[s : s + 1, col : col + chunk]
            f_ref[:, s * width + col : s * width + col + chunk] = cosine(angle, scale).astype(BF)
    lane = lax.axis_index("x") * 128
    upper, lower = split_two(r_ref[...].T)
    left = [upper, lower]
    for s in range(STEPS):
        left.append(f_ref[:, pl.ds(pl.multiple_of(s * width + lane, 128), 128)].T)
    left = jnp.concatenate(left, axis=0)
    part = jnp.dot(left, f_ref[...], preferred_element_type=F32)

    @pl.when(step == 0)
    def _():
        acc_ref[...] = part

    @pl.when(step > 0)
    def _():
        acc_ref[...] += part

    @pl.when(step == pl.num_programs(0) - 1)
    def _():
        half = lax.axis_index("c") * 256
        for group, (row, first) in enumerate(((256, 0), (384, width), (384, 0))):
            for side in range(2):
                lanes = pl.ds(pl.multiple_of(first + half + side * 128, 128), 128)
                block = acc_ref[row : row + 128, lanes]
                out_ref[side * 16 : side * 16 + 16, group * 8 : group * 8 + 8, :] = block.reshape(16, 8, 128)
        cross = acc_ref[0:128, :] + acc_ref[128:256, :]
        out_ref[:, 24:56, :] = cross.T.reshape(32, 32, 128)


def features(pieces, embeddings, shifts, residuals):
    total, depth = embeddings.shape
    width = shifts.shape[1]
    tile = 512
    whole = pl.BlockSpec(memory_space=pltpu.VMEM)
    return pl.pallas_call(
        feature_kernel,
        grid=(total // tile,),
        in_specs=[whole] * 8
        + [
            pl.BlockSpec((tile, depth), lambda i: (i, 0)),
            whole,
            pl.BlockSpec((tile, 128), lambda i: (i, 0)),
        ],
        out_specs=[pl.BlockSpec((tile, STEPS * width), lambda i: (i, 0)), whole],
        out_shape=[
            jax.ShapeDtypeStruct((total, STEPS * width), BF),
            jax.ShapeDtypeStruct((32, 56, 128), F32),
        ],
        scratch_shapes=[pltpu.VMEM((STEPS, depth, width), BF), pltpu.VMEM((512, STEPS * width), F32)],
        compiler_params=pltpu.CompilerParams(vmem_limit_bytes=52 << 20),
        name="features",
    )(*pieces, embeddings, shifts, residuals)


def times(upper, lower, values):
    high, low = split_two(values)
    both = jnp.dot(upper, jnp.concatenate([high, low], axis=1), preferred_element_type=F32)
    return both[:, :128] + both[:, 128:] + jnp.dot(lower, high, preferred_element_type=F32)


def conjugate_gradients(upper_ref, lower_ref, right, ridge):
    size = jnp.sum(right * right, axis=0, keepdims=True)
    floor = size * (TOLERANCE * TOLERANCE)

    def one(x, r, p, rr):
        ap = times(upper_ref[...], lower_ref[...], p) + ridge * p
        curve = jnp.sum(p * ap, axis=0, keepdims=True)
        alpha = jnp.where(curve > 0.0, rr / curve, 0.0)
        x = x + alpha * p
        r = r - alpha * ap
        new = jnp.sum(r * r, axis=0, keepdims=True)
        beta = jnp.where(rr > 0.0, new / rr, 0.0)
        return x, r, r + beta * p, new

    def body(state):
        count, x, r, p, rr = state
        for _ in range(2):
            x, r, p, rr = one(x, r, p, rr)
        return count + 1, x, r, p, rr

    def open_still(state):
        return jnp.logical_and(state[0] < MAX_LOOPS, jnp.max(state[4] - floor) > 0.0)

    state = (jnp.int32(0), jnp.zeros_like(right), right, right, size)
    return lax.while_loop(open_still, body, state)[1]


def solve_kernel(ridge, *refs):
    pieces = refs[:8]
    cross_ref, old_ref, f_hbm, r_hbm, coef_ref, out_ref, upper, lower, f_ref, r_ref, sems = refs[8:]
    loads = [
        pltpu.make_async_copy(f_hbm, f_ref, sems.at[0]),
        pltpu.make_async_copy(r_hbm, r_ref, sems.at[1]),
    ]
    for load in loads:
        load.start()
    for shift in range(4):
        for other in range(2):
            ref = pieces[shift * 2 + other]
            px, pc = offsets(shift, other)
            row = pl.multiple_of(px * 128, 128)
            for group in range(3):
                for side in range(2):
                    lanes = pl.ds(pl.multiple_of(pc * 256 + side * 128, 128), 128)
                    block = ref[side * 16 : side * 16 + 16, group * 8 : group * 8 + 8, :].reshape(128, 128)
                    high, low = split_two(block)
                    upper[group, pl.ds(row, 128), lanes] = high
                    lower[group, pl.ds(row, 128), lanes] = low
    cross = cross_ref[...].reshape(1024, 128)
    first = conjugate_gradients(upper.at[0], lower.at[0], cross[:512] - ridge * old_ref[0], ridge)
    coef_ref[0] = old_ref[0] + first
    cross = cross[512:] - times(upper[2], lower[2], first)
    second = conjugate_gradients(upper.at[1], lower.at[1], cross - ridge * old_ref[1], ridge)
    coef_ref[1] = old_ref[1] + second
    high, low = split_two(jnp.concatenate([first, second], axis=0))
    delta = jnp.concatenate([high, low], axis=1)
    tile = 256
    for load in loads:
        load.wait()
    for row in range(0, f_ref.shape[0], tile):
        both = jnp.dot(f_ref[row : row + tile, :], delta, preferred_element_type=F32)
        out_ref[row : row + tile, :] = r_ref[row : row + tile, :] - both[:, :128] - both[:, 128:]


def solve(pieces, cross, old, feats, residuals, ridge):
    def full(array):
        return pl.BlockSpec(array.shape, lambda: (0,) * array.ndim)

    return pl.pallas_call(
        functools.partial(solve_kernel, ridge),
        in_specs=[full(piece) for piece in pieces]
        + [full(cross), full(old), pl.BlockSpec(memory_space=pl.ANY), pl.BlockSpec(memory_space=pl.ANY)],
        out_specs=[full(old), full(residuals)],
        out_shape=[
            jax.ShapeDtypeStruct(old.shape, F32),
            jax.ShapeDtypeStruct(residuals.shape, F32),
        ],
        scratch_shapes=[
            pltpu.VMEM((3, 512, 512), BF),
            pltpu.VMEM((3, 512, 512), BF),
            pltpu.VMEM(feats.shape, BF),
            pltpu.VMEM(residuals.shape, F32),
            pltpu.SemaphoreType.DMA((2,)),
        ],
        compiler_params=pltpu.CompilerParams(vmem_limit_bytes=36 << 20),
        name="solve",
    )(*pieces, cross, old, feats, residuals)


def exchange(values, axes):
    return lax.all_to_all(values, axes, split_axis=0, concat_axis=0, tiled=True)


def gather(values, axes, count):
    return exchange(jnp.broadcast_to(values[None], (count,) + values.shape), axes)


def spread(values):
    nx, nc = lax.axis_size("x"), lax.axis_size("c")
    moved = [values]
    for shift in range(1, nx):
        moved.append(lax.ppermute(values, "x", [(i, (i + shift) % nx) for i in range(nx)]))
    pieces = []
    for value in moved:
        pieces += [value, lax.ppermute(value, "c", [(i, (i + 1) % nc) for i in range(nc)])]
    return pieces


def body(embeddings, residuals, projections, phases, old_coef, block_order):
    local_blocks, depth, width = projections.shape
    nrows = lax.axis_size("z") * lax.axis_size("y")
    ridge = 0.25 * (embeddings.shape[0] * nrows) / width

    got = exchange(payload(block_order, projections, phases, nrows), ROWS)
    copies, shifts = pick(block_order, got, local_blocks)
    weights = spread(exchange(copies, ROWS))
    feats, parts = features(weights, embeddings, shifts, residuals)

    summed = jnp.sum(exchange(parts, ROWS), axis=0)
    grams = gather(summed[:24], ROWS, nrows)
    cross, grams = lax.optimization_barrier((summed[24:], grams))
    pieces = spread(grams)
    cross = gather(cross, ROWS, nrows)
    coef, current = solve(pieces, cross, old_coef, feats, residuals, ridge)
    return current, coef


def solution(mesh):
    grid = Mesh(mesh.devices.reshape(8, 4, 4, 2), ROWS + CLS)
    in_specs = (
        P(ROWS, None),
        P(ROWS, CLS),
        P(ROWS, None, None),
        P(ROWS, None),
        P(None, None, CLS),
        P(),
    )
    out_specs = (P(ROWS, CLS), P(None, None, CLS))
    return jax.shard_map(body, mesh=grid, in_specs=in_specs, out_specs=out_specs, check_vma=False)
```

```python
import functools
import math

import jax
import jax.numpy as jnp
from jax import lax
from jax.experimental import pallas as pl
from jax.experimental.pallas import tpu as pltpu
from jax.sharding import Mesh
from jax.sharding import PartitionSpec as P

STEPS = 2
BF = jnp.bfloat16
F32 = jnp.float32
ROWS = ("z", "y")
CLS = ("x", "c")

SINE = (6.28316404416301, -41.33714234877015, 81.3407680297695, -70.99342411797343)
TOLERANCE = 5e-5
MAX_LOOPS = 2000
UNROLL = 2


def cosine(angle, scale):
    turns = angle * (1.0 / (2.0 * math.pi))
    offset = turns - lax.round(turns, lax.RoundingMethod.TO_NEAREST_EVEN)
    q = 0.25 - jnp.abs(offset)
    z = q * q
    total = SINE[-1] * scale
    for coefficient in SINE[-2::-1]:
        total = total * z + coefficient * scale
    return total * q


def split_two(values):
    upper = values.astype(BF)
    return upper, (values - upper.astype(F32)).astype(BF)


def offsets(shift, other):
    return lax.rem(lax.axis_index("x") + 4 - shift, 4), lax.rem(lax.axis_index("c") + other, 2)


def payload_kernel(local_blocks, order, proj_ref, phase_ref, out_ref):
    part = 128
    width = proj_ref.shape[2]
    share = out_ref.shape[0] // STEPS
    at = pl.multiple_of((lax.axis_index("x") * 2 + lax.axis_index("c")) * part, part)
    for s in range(STEPS):
        slot = lax.rem(order[s], local_blocks)
        mine = proj_ref[pl.ds(slot, 1), pl.ds(at, part), :]
        out_ref[s * share : (s + 1) * share, :, :width] = mine.reshape(share, part // share, width)
    bands = []
    for s in range(STEPS):
        slot = lax.rem(order[s], local_blocks)
        shift = phase_ref[0:1, :].astype(F32)
        for k in range(1, phase_ref.shape[0]):
            shift = jnp.where(slot == k, phase_ref[k : k + 1, :].astype(F32), shift)
        bands += [shift[:, q * 128 : (q + 1) * 128] for q in range(width // 128)]
    band = jnp.concatenate(bands, axis=0).astype(BF)
    out_ref[:, :, width:] = jnp.broadcast_to(band[None], (out_ref.shape[0],) + band.shape)


def payload(order, projections, phases, nrows):
    local_blocks, depth, width = projections.shape
    whole = pl.BlockSpec(memory_space=pltpu.VMEM)
    return pl.pallas_call(
        functools.partial(payload_kernel, local_blocks),
        in_specs=[pl.BlockSpec(memory_space=pltpu.SMEM), whole, whole],
        out_specs=whole,
        out_shape=jax.ShapeDtypeStruct((nrows, 8, width + 128), BF),
        name="payload",
    )(order, projections, phases)


def pick_kernel(local_blocks, order, got_ref, piece_ref, shift_ref):
    nrows, _, width = piece_ref.shape
    row = lax.axis_index("z") * 4 + lax.axis_index("y")
    source = jnp.where(row < nrows // STEPS, order[0], order[1]) // local_blocks
    piece = got_ref[pl.ds(source, 1), :, :width]
    piece_ref[...] = jnp.broadcast_to(piece, piece_ref.shape)
    for s in range(STEPS):
        band = got_ref[pl.ds(order[s] // local_blocks, 1), :, width:][0].astype(F32)
        for q in range(width // 128):
            row = s * (width // 128) + q
            shift_ref[s : s + 1, q * 128 : (q + 1) * 128] = band[row : row + 1, :]


def pick(order, got, local_blocks):
    nrows, eight, wide = got.shape
    width = wide - 128
    whole = pl.BlockSpec(memory_space=pltpu.VMEM)
    return pl.pallas_call(
        functools.partial(pick_kernel, local_blocks),
        in_specs=[pl.BlockSpec(memory_space=pltpu.SMEM), whole],
        out_specs=[whole, whole],
        out_shape=[
            jax.ShapeDtypeStruct((nrows, eight, width), BF),
            jax.ShapeDtypeStruct((STEPS, width), F32),
        ],
        name="pick",
    )(order, got)


def feature_kernel(*refs):
    pieces = refs[:8]
    e_ref, shift_ref, r_ref, f_ref, out_ref, w_ref, left_ref, all_ref = refs[8:]
    step = pl.program_id(0)
    width = w_ref.shape[2]
    scale = 1.0 / width**0.5

    @pl.when(step == 0)
    def _():
        for shift in range(4):
            for other in range(2):
                px, pc = offsets(shift, other)
                at = pl.multiple_of(px * 256 + pc * 128, 128)
                for s in range(STEPS):
                    part = pieces[shift * 2 + other][s * 16 : s * 16 + 16, :, :]
                    w_ref[s, pl.ds(at, 128), :] = part.reshape(128, width)

    spots = [
        (row, s, col)
        for row in range(0, e_ref.shape[0], 512)
        for s in range(STEPS)
        for col in range(0, width, 256)
    ]

    def angles(row, s, col):
        return jnp.dot(e_ref[row : row + 512, :], w_ref[s, :, col : col + 256], preferred_element_type=F32)

    ahead = [angles(*spot) for spot in spots[:1]]
    for index, (row, s, col) in enumerate(spots):
        if index + 1 < len(spots):
            ahead.append(angles(*spots[index + 1]))
        angle = ahead.pop(0) + shift_ref[s : s + 1, col : col + 256]
        f_ref[row : row + 512, s * width + col : s * width + col + 256] = cosine(angle, scale).astype(BF)
    lane = lax.axis_index("x") * 128
    upper, lower = split_two(r_ref[...].T)
    left = [upper, lower]
    for s in range(STEPS):
        left.append(f_ref[:, pl.ds(pl.multiple_of(s * width + lane, 128), 128)].T)
    rows = e_ref.shape[0]
    here = pl.multiple_of(step * rows, rows)
    left_ref[:, pl.ds(here, rows)] = jnp.concatenate(left, axis=0)
    all_ref[pl.ds(here, rows), :] = f_ref[...]

    @pl.when(step == pl.num_programs(0) - 1)
    def _():
        half = lax.axis_index("c")

        def products(n, count):
            right = all_ref[:, n * 256 : n * 256 + 256]
            part = jnp.dot(left_ref[:count, :], right, preferred_element_type=F32)
            cross = part[0:128] + part[128:256]
            out_ref[n * 8 : n * 8 + 8, 24:56, :] = cross.T.reshape(8, 32, 128)
            return part

        for n in range(4):

            @pl.when(half == n % 2)
            def _():
                part = products(n, 512)
                for group, row in ((0, 256), (2, 384)) if n < 2 else ((1, 384),):
                    for side in range(2):
                        block = part[row : row + 128, side * 128 : side * 128 + 128].reshape(16, 8, 128)
                        out_ref[side * 16 : side * 16 + 16, group * 8 : group * 8 + 8, :] = block

            @pl.when(half != n % 2)
            def _():
                products(n, 256)


def features(pieces, embeddings, shifts, residuals):
    total, depth = embeddings.shape
    width = shifts.shape[1]
    tile = 512
    whole = pl.BlockSpec(memory_space=pltpu.VMEM)
    return pl.pallas_call(
        feature_kernel,
        grid=(total // tile,),
        in_specs=[whole] * 8
        + [
            pl.BlockSpec((tile, depth), lambda i: (i, 0)),
            whole,
            pl.BlockSpec((tile, 128), lambda i: (i, 0)),
        ],
        out_specs=[pl.BlockSpec((tile, STEPS * width), lambda i: (i, 0)), whole],
        out_shape=[
            jax.ShapeDtypeStruct((total, STEPS * width), BF),
            jax.ShapeDtypeStruct((32, 56, 128), F32),
        ],
        scratch_shapes=[
            pltpu.VMEM((STEPS, depth, width), BF),
            pltpu.VMEM((512, total), BF),
            pltpu.VMEM((total, STEPS * width), BF),
        ],
        compiler_params=pltpu.CompilerParams(vmem_limit_bytes=52 << 20),
        name="features",
    )(*pieces, embeddings, shifts, residuals)


def times(upper, lower, values):
    high, low = split_two(values)
    both = jnp.dot(upper, jnp.concatenate([high, low], axis=1), preferred_element_type=F32)
    return both[:, :128] + both[:, 128:] + jnp.dot(lower, high, preferred_element_type=F32)


def folded(values):
    part = [values[row : row + 8] for row in range(0, values.shape[0], 8)]
    while len(part) > 1:
        part = [part[i] + part[i + 1] for i in range(0, len(part), 2)]
    return part[0]


def total(parts):
    while len(parts) > 1:
        parts = [parts[i] + parts[i + 1] for i in range(0, len(parts), 2)]
    return jnp.sum(parts[0], axis=0, keepdims=True)


def conjugate_gradients(upper_ref, lower_ref, x_ref, r_ref, p_ref, ap_ref, parts_ref, ridge):
    n = r_ref.shape[0]
    bound = (TOLERANCE * ridge) ** 2
    bands = [slice(row, row + 128) for row in range(0, n, 128)]

    def direct(band, p):
        p_ref[band] = p
        high, low = split_two(p)
        parts_ref[band, :128] = high
        parts_ref[band, 128:] = low

    def one(rr):
        sums = []
        for row in range(0, n, 512):
            band = slice(row, row + 512)
            both = jnp.dot(upper_ref[band, :], parts_ref[...], preferred_element_type=F32)
            rest = jnp.dot(lower_ref[band, :], parts_ref[:, :128], preferred_element_type=F32)
            p = p_ref[band]
            ap = both[:, :128] + both[:, 128:] + rest + ridge * p
            ap_ref[band] = ap
            sums.append(folded(p * ap))
        curve = total(sums)
        alpha = jnp.where(curve > 0.0, rr / curve, 0.0)
        sums = []
        for band in bands:
            r = r_ref[band] - alpha * ap_ref[band]
            r_ref[band] = r
            sums.append(folded(r * r))
        new = total(sums)
        beta = jnp.where(rr > 0.0, new / rr, 0.0)
        for band in bands:
            p = p_ref[band]
            x_ref[band] += alpha * p
            direct(band, r_ref[band] + beta * p)
        return new

    def open_still(state):
        return jnp.logical_and(state[0] < MAX_LOOPS, state[1] > 0.0)

    def body(state):
        rr = state[2]
        for _ in range(UNROLL):
            rr = one(rr)
        size = total([folded(x_ref[band] * x_ref[band]) for band in bands])
        return state[0] + 1, jnp.max(rr - bound * size), rr

    for band in bands:
        x_ref[band] = jnp.zeros_like(r_ref[band])
        direct(band, r_ref[band])
    size = total([folded(r_ref[band] * r_ref[band]) for band in bands])
    lax.while_loop(open_still, body, (jnp.int32(0), jnp.float32(1.0), size))


def solve_kernel(ridge, *refs):
    pieces = refs[:8]
    cross_ref, old_ref, f_hbm, r_hbm, coef_ref, out_ref, upper, lower, f_ref, r_ref, x_ref, res_ref, p_ref, ap_ref, parts_ref, delta_ref, sems = refs[8:]
    loads = [
        pltpu.make_async_copy(f_hbm, f_ref, sems.at[0]),
        pltpu.make_async_copy(r_hbm, r_ref, sems.at[1]),
    ]
    for load in loads:
        load.start()
    for shift in range(4):
        for other in range(2):
            ref = pieces[shift * 2 + other]
            px, pc = offsets(shift, other)
            row = pl.multiple_of(px * 128, 128)
            for group in range(3):
                for side in range(2):
                    lanes = pl.ds(pl.multiple_of(pc * 256 + side * 128, 128), 128)
                    block = ref[side * 16 : side * 16 + 16, group * 8 : group * 8 + 8, :].reshape(128, 128)
                    high, low = split_two(block)
                    upper[group, pl.ds(row, 128), lanes] = high
                    lower[group, pl.ds(row, 128), lanes] = low
    n = upper.shape[1]
    per = 32 // STEPS
    work = (x_ref, res_ref, p_ref, ap_ref, parts_ref)
    res_ref[...] = cross_ref[:per].reshape(n, 128) - ridge * old_ref[0]
    conjugate_gradients(upper.at[0], lower.at[0], *work, ridge)
    first = x_ref[...]
    coef_ref[0] = old_ref[0] + first
    res_ref[...] = cross_ref[per:].reshape(n, 128) - ridge * old_ref[1] - times(upper[2], lower[2], first)
    high_first, low_first = split_two(first)
    delta_ref[:n, :128] = high_first
    delta_ref[:n, 128:] = low_first
    conjugate_gradients(upper.at[1], lower.at[1], *work, ridge)
    second = x_ref[...]
    coef_ref[1] = old_ref[1] + second
    high, low = split_two(second)
    delta_ref[n:, :128] = high
    delta_ref[n:, 128:] = low
    delta = delta_ref[...]
    tile = 256
    for load in loads:
        load.wait()
    for row in range(0, f_ref.shape[0], tile):
        both = jnp.dot(f_ref[row : row + tile, :], delta, preferred_element_type=F32)
        out_ref[row : row + tile, :] = r_ref[row : row + tile, :] - both[:, :128] - both[:, 128:]


def solve(pieces, cross, old, feats, residuals, ridge):
    def full(array):
        return pl.BlockSpec(array.shape, lambda: (0,) * array.ndim)

    return pl.pallas_call(
        functools.partial(solve_kernel, ridge),
        in_specs=[full(piece) for piece in pieces]
        + [full(cross), full(old), pl.BlockSpec(memory_space=pl.ANY), pl.BlockSpec(memory_space=pl.ANY)],
        out_specs=[full(old), full(residuals)],
        out_shape=[
            jax.ShapeDtypeStruct(old.shape, F32),
            jax.ShapeDtypeStruct(residuals.shape, F32),
        ],
        scratch_shapes=[
            pltpu.VMEM((3, 512, 512), BF),
            pltpu.VMEM((3, 512, 512), BF),
            pltpu.VMEM(feats.shape, BF),
            pltpu.VMEM(residuals.shape, F32),
            pltpu.VMEM((512, 128), F32),
            pltpu.VMEM((512, 128), F32),
            pltpu.VMEM((512, 128), F32),
            pltpu.VMEM((512, 128), F32),
            pltpu.VMEM((512, 256), BF),
            pltpu.VMEM((1024, 256), BF),
            pltpu.SemaphoreType.DMA((2,)),
        ],
        compiler_params=pltpu.CompilerParams(vmem_limit_bytes=52 << 20),
        name="solve",
    )(*pieces, cross, old, feats, residuals)


def exchange(values, axes):
    return lax.all_to_all(values, axes, split_axis=0, concat_axis=0, tiled=True)


def gather(values, axes, count):
    return exchange(jnp.broadcast_to(values[None], (count,) + values.shape), axes)


def spread(values):
    nx, nc = lax.axis_size("x"), lax.axis_size("c")
    moved = [values]
    for shift in range(1, nx):
        moved.append(lax.ppermute(values, "x", [(i, (i + shift) % nx) for i in range(nx)]))
    pieces = []
    for value in moved:
        pieces += [value, lax.ppermute(value, "c", [(i, (i + 1) % nc) for i in range(nc)])]
    return pieces


def body(embeddings, residuals, projections, phases, old_coef, block_order):
    local_blocks, depth, width = projections.shape
    nrows = lax.axis_size("z") * lax.axis_size("y")
    ridge = 0.25 * (embeddings.shape[0] * nrows) / width

    got = exchange(payload(block_order, projections, phases, nrows), ROWS)
    copies, shifts = pick(block_order, got, local_blocks)
    weights = spread(exchange(copies, ROWS))
    feats, parts = features(weights, embeddings, shifts, residuals)

    summed = jnp.sum(exchange(parts, ROWS), axis=0)
    grams = gather(summed[:24], ROWS, nrows)
    cross, grams = lax.optimization_barrier((summed[24:], grams))
    pieces = spread(grams)
    cross = gather(cross, ROWS, nrows)
    coef, current = solve(pieces, cross, old_coef, feats, residuals, ridge)
    return current, coef


def solution(mesh):
    grid = Mesh(mesh.devices.reshape(8, 4, 4, 2), ROWS + CLS)
    in_specs = (
        P(ROWS, None),
        P(ROWS, CLS),
        P(ROWS, None, None),
        P(ROWS, None),
        P(None, None, CLS),
        P(),
    )
    out_specs = (P(ROWS, CLS), P(None, None, CLS))
    return jax.shard_map(body, mesh=grid, in_specs=in_specs, out_specs=out_specs, check_vma=False)
```

```python
import functools
import math

import jax
import jax.numpy as jnp
from jax import lax
from jax.experimental import pallas as pl
from jax.experimental.pallas import tpu as pltpu
from jax.sharding import Mesh
from jax.sharding import PartitionSpec as P

STEPS = 2
BF = jnp.bfloat16
F32 = jnp.float32
ROWS = ("z", "y")
CLS = ("x", "c")

SINE = (6.28316404416301, -41.33714234877015, 81.3407680297695, -70.99342411797343)
TOLERANCE = 5e-5
MAX_LOOPS = 2000
UNROLL = 2


def cosine(angle, scale):
    turns = angle * (1.0 / (2.0 * math.pi))
    offset = turns - lax.round(turns, lax.RoundingMethod.TO_NEAREST_EVEN)
    q = 0.25 - jnp.abs(offset)
    z = q * q
    total = SINE[-1] * scale
    for coefficient in SINE[-2::-1]:
        total = total * z + coefficient * scale
    return total * q


def split_two(values):
    upper = values.astype(BF)
    return upper, (values - upper.astype(F32)).astype(BF)


def offsets(shift, other):
    return lax.rem(lax.axis_index("x") + 4 - shift, 4), lax.rem(lax.axis_index("c") + other, 2)


def payload_kernel(local_blocks, order, proj_ref, phase_ref, out_ref):
    part = 128
    width = proj_ref.shape[2]
    share = out_ref.shape[0] // STEPS
    at = pl.multiple_of((lax.axis_index("x") * 2 + lax.axis_index("c")) * part, part)
    for s in range(STEPS):
        slot = lax.rem(order[s], local_blocks)
        mine = proj_ref[pl.ds(slot, 1), pl.ds(at, part), :]
        out_ref[s * share : (s + 1) * share, :, :width] = mine.reshape(share, part // share, width)
    bands = []
    for s in range(STEPS):
        slot = lax.rem(order[s], local_blocks)
        shift = phase_ref[0:1, :].astype(F32)
        for k in range(1, phase_ref.shape[0]):
            shift = jnp.where(slot == k, phase_ref[k : k + 1, :].astype(F32), shift)
        bands += [shift[:, q * 128 : (q + 1) * 128] for q in range(width // 128)]
    band = jnp.concatenate(bands, axis=0).astype(BF)
    out_ref[:, :, width:] = jnp.broadcast_to(band[None], (out_ref.shape[0],) + band.shape)


def payload(order, projections, phases, nrows):
    local_blocks, depth, width = projections.shape
    whole = pl.BlockSpec(memory_space=pltpu.VMEM)
    return pl.pallas_call(
        functools.partial(payload_kernel, local_blocks),
        in_specs=[pl.BlockSpec(memory_space=pltpu.SMEM), whole, whole],
        out_specs=whole,
        out_shape=jax.ShapeDtypeStruct((nrows, 8, width + 128), BF),
        name="payload",
    )(order, projections, phases)


def pick_kernel(local_blocks, order, got_ref, piece_ref, shift_ref):
    nrows, _, width = piece_ref.shape
    row = lax.axis_index("z") * 4 + lax.axis_index("y")
    source = jnp.where(row < nrows // STEPS, order[0], order[1]) // local_blocks
    piece = got_ref[pl.ds(source, 1), :, :width]
    piece_ref[...] = jnp.broadcast_to(piece, piece_ref.shape)
    for s in range(STEPS):
        band = got_ref[pl.ds(order[s] // local_blocks, 1), :, width:][0].astype(F32)
        for q in range(width // 128):
            row = s * (width // 128) + q
            shift_ref[s : s + 1, q * 128 : (q + 1) * 128] = band[row : row + 1, :]


def pick(order, got, local_blocks):
    nrows, eight, wide = got.shape
    width = wide - 128
    whole = pl.BlockSpec(memory_space=pltpu.VMEM)
    return pl.pallas_call(
        functools.partial(pick_kernel, local_blocks),
        in_specs=[pl.BlockSpec(memory_space=pltpu.SMEM), whole],
        out_specs=[whole, whole],
        out_shape=[
            jax.ShapeDtypeStruct((nrows, eight, width), BF),
            jax.ShapeDtypeStruct((STEPS, width), F32),
        ],
        name="pick",
    )(order, got)


def feature_kernel(s, *refs):
    pieces = refs[:8]
    if s:
        f_before, refs = refs[11], refs[:11] + refs[12:]
    e_ref, shift_ref, r_ref, f_ref, out_ref, w_ref, left_ref, all_ref = refs[8:]
    step = pl.program_id(0)
    width = w_ref.shape[1]
    scale = 1.0 / width**0.5

    @pl.when(step == 0)
    def _():
        for shift in range(4):
            for other in range(2):
                px, pc = offsets(shift, other)
                at = pl.multiple_of(px * 256 + pc * 128, 128)
                part = pieces[shift * 2 + other][s * 16 : s * 16 + 16, :, :]
                w_ref[pl.ds(at, 128), :] = part.reshape(128, width)

    cols = range(0, width, 256)
    rows = e_ref.shape[0]
    ahead = [jnp.dot(e_ref[...], w_ref[:, col : col + 256], preferred_element_type=F32) for col in cols]
    for col, angle in zip(cols, ahead):
        angle = angle + shift_ref[s : s + 1, col : col + 256]
        f_ref[:, col : col + 256] = cosine(angle, scale).astype(BF)
    lane = pl.multiple_of(lax.axis_index("x") * 128, 128)
    upper, lower = split_two(r_ref[...].T)
    here = pl.multiple_of(step * rows, rows)
    left_ref[:, pl.ds(here, rows)] = jnp.concatenate([upper, lower, f_ref[:, pl.ds(lane, 128)].T], axis=0)
    all_ref[pl.ds(here, rows), :] = f_ref[...]

    @pl.when(step == pl.num_programs(0) - 1)
    def _():
        half = lax.axis_index("c")
        first = 16 if s else 8

        def gram(part, row):
            for side in range(2):
                block = part[:, side * 128 : side * 128 + 128].reshape(16, 8, 128)
                out_ref[side * 16 : side * 16 + 16, row : row + 8, :] = block

        def products(n, count):
            right = all_ref[:, n * 256 : n * 256 + 256]
            part = jnp.dot(left_ref[:count, :], right, preferred_element_type=F32)
            cross = part[0:128] + part[128:256]
            out_ref[n * 16 : n * 16 + 16, first : first + 16, :] = cross.T.reshape(16, 16, 128)
            return part

        for n in range(2):

            @pl.when(half == n)
            def _():
                part = products(n, 384)
                gram(part[256:384], 0)

            @pl.when(half != n)
            def _():
                products(n, 256)

        if s:
            right = f_before[:, pl.ds(pl.multiple_of(half * 256, 256), 256)]
            gram(jnp.dot(left_ref[256:384, :], right, preferred_element_type=F32), 8)


def features(s, pieces, embeddings, shifts, residuals, before=()):
    total, depth = embeddings.shape
    width = shifts.shape[1]
    tile = 512
    count = 32 if s else 24
    whole = pl.BlockSpec(memory_space=pltpu.VMEM)
    return pl.pallas_call(
        functools.partial(feature_kernel, s),
        grid=(total // tile,),
        in_specs=[whole] * 8
        + [
            pl.BlockSpec((tile, depth), lambda i: (i, 0)),
            whole,
            pl.BlockSpec((tile, 128), lambda i: (i, 0)),
        ]
        + [pl.BlockSpec((total, width), lambda i: (0, 0)) for _ in before],
        out_specs=[pl.BlockSpec((tile, width), lambda i: (i, 0)), whole],
        out_shape=[
            jax.ShapeDtypeStruct((total, width), BF),
            jax.ShapeDtypeStruct((32, count, 128), F32),
        ],
        scratch_shapes=[
            pltpu.VMEM((depth, width), BF),
            pltpu.VMEM((384, total), BF),
            pltpu.VMEM((total, width), BF),
        ],
        compiler_params=pltpu.CompilerParams(vmem_limit_bytes=48 << 20),
        cost_estimate=pl.CostEstimate(flops=4 << 30, bytes_accessed=8 << 20, transcendentals=0),
        name="features",
    )(*pieces, embeddings, shifts, residuals, *before)


def times(upper, lower, values):
    high, low = split_two(values)
    both = jnp.dot(upper, jnp.concatenate([high, low], axis=1), preferred_element_type=F32)
    return both[:, :128] + both[:, 128:] + jnp.dot(lower, high, preferred_element_type=F32)


def folded(values):
    part = [values[row : row + 8] for row in range(0, values.shape[0], 8)]
    while len(part) > 1:
        part = [part[i] + part[i + 1] for i in range(0, len(part), 2)]
    return part[0]


def total(parts):
    while len(parts) > 1:
        parts = [parts[i] + parts[i + 1] for i in range(0, len(parts), 2)]
    return jnp.sum(parts[0], axis=0, keepdims=True)


def conjugate_gradients(upper_ref, lower_ref, x_ref, r_ref, p_ref, ap_ref, parts_ref, ridge):
    n = r_ref.shape[0]
    bound = (TOLERANCE * ridge) ** 2
    bands = [slice(row, row + 128) for row in range(0, n, 128)]

    def direct(band, p):
        p_ref[band] = p
        high, low = split_two(p)
        parts_ref[band, :128] = high
        parts_ref[band, 128:] = low

    def one(rr):
        sums = []
        for row in range(0, n, 512):
            band = slice(row, row + 512)
            both = jnp.dot(upper_ref[band, :], parts_ref[...], preferred_element_type=F32)
            rest = jnp.dot(lower_ref[band, :], parts_ref[:, :128], preferred_element_type=F32)
            p = p_ref[band]
            ap = both[:, :128] + both[:, 128:] + rest + ridge * p
            ap_ref[band] = ap
            sums.append(folded(p * ap))
        curve = total(sums)
        alpha = jnp.where(curve > 0.0, rr / curve, 0.0)
        sums = []
        for band in bands:
            r = r_ref[band] - alpha * ap_ref[band]
            r_ref[band] = r
            sums.append(folded(r * r))
        new = total(sums)
        beta = jnp.where(rr > 0.0, new / rr, 0.0)
        for band in bands:
            p = p_ref[band]
            x_ref[band] += alpha * p
            direct(band, r_ref[band] + beta * p)
        return new

    def open_still(state):
        return jnp.logical_and(state[0] < MAX_LOOPS, state[1] > 0.0)

    def body(state):
        rr = state[2]
        for _ in range(UNROLL):
            rr = one(rr)
        size = total([folded(x_ref[band] * x_ref[band]) for band in bands])
        return state[0] + 1, jnp.max(rr - bound * size), rr

    for band in bands:
        x_ref[band] = jnp.zeros_like(r_ref[band])
        direct(band, r_ref[band])
    size = total([folded(r_ref[band] * r_ref[band]) for band in bands])
    lax.while_loop(open_still, body, (jnp.int32(0), jnp.float32(1.0), size))


def solve_kernel(s, ridge, *refs):
    pieces = refs[:8]
    got_ref, old_ref, f_hbm, r_hbm = refs[8:12]
    refs = refs[12:]
    if s:
        before_ref, refs = refs[0], refs[1:]
    out_ref, delta_out, upper, lower, f_ref, r_ref, x_ref, res_ref, p_ref, ap_ref, parts_ref, sems = refs
    loads = [
        pltpu.make_async_copy(f_hbm, f_ref, sems.at[0]),
        pltpu.make_async_copy(r_hbm, r_ref, sems.at[1]),
    ]
    for load in loads:
        load.start()
    grams = s + 1
    for shift in range(4):
        for other in range(2):
            ref = pieces[shift * 2 + other]
            px, pc = offsets(shift, other)
            row = pl.multiple_of(px * 128, 128)
            for group in range(grams):
                for side in range(2):
                    lanes = pl.ds(pl.multiple_of(pc * 256 + side * 128, 128), 128)
                    block = ref[side * 16 : side * 16 + 16, group * 8 : group * 8 + 8, :].reshape(128, 128)
                    high, low = split_two(block)
                    upper[group, pl.ds(row, 128), lanes] = high
                    lower[group, pl.ds(row, 128), lanes] = low
    n = upper.shape[1]
    cross = got_ref[:, grams * 8 : grams * 8 + 16, :].reshape(n, 128) - ridge * old_ref[s]
    if s:
        cross = cross - times(upper[1], lower[1], before_ref[...])
    res_ref[...] = cross
    conjugate_gradients(upper.at[0], lower.at[0], x_ref, res_ref, p_ref, ap_ref, parts_ref, ridge)
    change = x_ref[...]
    if s:
        delta_out[0] = old_ref[0] + before_ref[...]
        delta_out[1] = old_ref[1] + change
    else:
        delta_out[...] = change
    high, low = split_two(change)
    delta = jnp.concatenate([high, low], axis=1)
    tile = 256
    for load in loads:
        load.wait()
    for row in range(0, f_ref.shape[0], tile):
        both = jnp.dot(f_ref[row : row + tile, :], delta, preferred_element_type=F32)
        out_ref[row : row + tile, :] = r_ref[row : row + tile, :] - both[:, :128] - both[:, 128:]


def solve(s, pieces, got, old, feats, residuals, ridge, before=()):
    def full(array):
        return pl.BlockSpec(array.shape, lambda: (0,) * array.ndim)

    second = jax.ShapeDtypeStruct(old.shape if s else old.shape[1:], F32)
    return pl.pallas_call(
        functools.partial(solve_kernel, s, ridge),
        in_specs=[full(piece) for piece in pieces]
        + [full(got), full(old), pl.BlockSpec(memory_space=pl.ANY), pl.BlockSpec(memory_space=pl.ANY)]
        + [full(array) for array in before],
        out_specs=[full(residuals), full(second)],
        out_shape=[jax.ShapeDtypeStruct(residuals.shape, F32), second],
        scratch_shapes=[
            pltpu.VMEM((s + 1, 512, 512), BF),
            pltpu.VMEM((s + 1, 512, 512), BF),
            pltpu.VMEM(feats.shape, BF),
            pltpu.VMEM(residuals.shape, F32),
            pltpu.VMEM((512, 128), F32),
            pltpu.VMEM((512, 128), F32),
            pltpu.VMEM((512, 128), F32),
            pltpu.VMEM((512, 128), F32),
            pltpu.VMEM((512, 256), BF),
            pltpu.SemaphoreType.DMA((2,)),
        ],
        compiler_params=pltpu.CompilerParams(vmem_limit_bytes=48 << 20),
        cost_estimate=pl.CostEstimate(flops=8 << 30, bytes_accessed=8 << 20, transcendentals=0),
        name="solve",
    )(*pieces, got, old, feats, residuals, *before)


def exchange(values, axes):
    return lax.all_to_all(values, axes, split_axis=0, concat_axis=0, tiled=True)


def gather(values, axes, count):
    return exchange(jnp.broadcast_to(values[None], (count,) + values.shape), axes)


def spread(values):
    nx, nc = lax.axis_size("x"), lax.axis_size("c")
    moved = [values]
    for shift in range(1, nx):
        moved.append(lax.ppermute(values, "x", [(i, (i + shift) % nx) for i in range(nx)]))
    pieces = []
    for value in moved:
        pieces += [value, lax.ppermute(value, "c", [(i, (i + 1) % nc) for i in range(nc)])]
    return pieces


def body(embeddings, residuals, projections, phases, old_coef, block_order):
    local_blocks, depth, width = projections.shape
    nrows = lax.axis_size("z") * lax.axis_size("y")
    ridge = 0.25 * (embeddings.shape[0] * nrows) / width

    got = exchange(payload(block_order, projections, phases, nrows), ROWS)
    copies, shifts = pick(block_order, got, local_blocks)
    weights = spread(exchange(copies, ROWS))
    feats_a, parts_a = features(0, weights, embeddings, shifts, residuals)
    feats_b, parts_b = features(1, weights, embeddings, shifts, residuals, (feats_a,))

    got_a = gather(jnp.sum(exchange(parts_a, ROWS), axis=0), ROWS, nrows)
    got_b = gather(jnp.sum(exchange(parts_b, ROWS), axis=0), ROWS, nrows)
    current, change = solve(0, spread(got_a[:, :8]), got_a, old_coef, feats_a, residuals, ridge)
    current, coef = solve(1, spread(got_b[:, :16]), got_b, old_coef, feats_b, current, ridge, (change,))
    return current, coef


def solution(mesh):
    grid = Mesh(mesh.devices.reshape(8, 4, 4, 2), ROWS + CLS)
    in_specs = (
        P(ROWS, None),
        P(ROWS, CLS),
        P(ROWS, None, None),
        P(ROWS, None),
        P(None, None, CLS),
        P(),
    )
    out_specs = (P(ROWS, CLS), P(None, None, CLS))
    return jax.shard_map(body, mesh=grid, in_specs=in_specs, out_specs=out_specs, check_vma=False)
```

```python
import functools
import math

import jax
import jax.numpy as jnp
from jax import lax
from jax.experimental import pallas as pl
from jax.experimental.pallas import tpu as pltpu
from jax.sharding import Mesh
from jax.sharding import PartitionSpec as P

STEPS = 2
BF = jnp.bfloat16
F32 = jnp.float32
ROWS = ("z", "y")
CLS = ("x", "c")

SINE = (6.28316404416301, -41.33714234877015, 81.3407680297695, -70.99342411797343)
TOLERANCE = 5e-5
MAX_LOOPS = 2000
UNROLL = 2


def cosine(angle, scale):
    turns = angle * (1.0 / (2.0 * math.pi))
    offset = turns - lax.round(turns, lax.RoundingMethod.TO_NEAREST_EVEN)
    q = 0.25 - jnp.abs(offset)
    z = q * q
    total = SINE[-1] * scale
    for coefficient in SINE[-2::-1]:
        total = total * z + coefficient * scale
    return total * q


def split_two(values):
    upper = values.astype(BF)
    return upper, (values - upper.astype(F32)).astype(BF)


def offsets(shift, other):
    return lax.rem(lax.axis_index("x") + 4 - shift, 4), lax.rem(lax.axis_index("c") + other, 2)


def payload_kernel(local_blocks, order, proj_ref, phase_ref, out_ref):
    part = 128
    width = proj_ref.shape[2]
    share = out_ref.shape[0] // STEPS
    at = pl.multiple_of((lax.axis_index("x") * 2 + lax.axis_index("c")) * part, part)
    for s in range(STEPS):
        slot = lax.rem(order[s], local_blocks)
        mine = proj_ref[pl.ds(slot, 1), pl.ds(at, part), :]
        out_ref[s * share : (s + 1) * share, :, :width] = mine.reshape(share, part // share, width)
    bands = []
    for s in range(STEPS):
        slot = lax.rem(order[s], local_blocks)
        shift = phase_ref[0:1, :].astype(F32)
        for k in range(1, phase_ref.shape[0]):
            shift = jnp.where(slot == k, phase_ref[k : k + 1, :].astype(F32), shift)
        bands += [shift[:, q * 128 : (q + 1) * 128] for q in range(width // 128)]
    band = jnp.concatenate(bands, axis=0).astype(BF)
    out_ref[:, :, width:] = jnp.broadcast_to(band[None], (out_ref.shape[0],) + band.shape)


def payload(order, projections, phases, nrows):
    local_blocks, depth, width = projections.shape
    whole = pl.BlockSpec(memory_space=pltpu.VMEM)
    return pl.pallas_call(
        functools.partial(payload_kernel, local_blocks),
        in_specs=[pl.BlockSpec(memory_space=pltpu.SMEM), whole, whole],
        out_specs=whole,
        out_shape=jax.ShapeDtypeStruct((nrows, 8, width + 128), BF),
        name="payload",
    )(order, projections, phases)


def pick_kernel(local_blocks, order, got_ref, piece_ref, shift_ref):
    nrows, _, width = piece_ref.shape
    row = lax.axis_index("z") * 4 + lax.axis_index("y")
    source = jnp.where(row < nrows // STEPS, order[0], order[1]) // local_blocks
    piece = got_ref[pl.ds(source, 1), :, :width]
    piece_ref[...] = jnp.broadcast_to(piece, piece_ref.shape)
    for s in range(STEPS):
        band = got_ref[pl.ds(order[s] // local_blocks, 1), :, width:][0].astype(F32)
        for q in range(width // 128):
            row = s * (width // 128) + q
            shift_ref[s : s + 1, q * 128 : (q + 1) * 128] = band[row : row + 1, :]


def pick(order, got, local_blocks):
    nrows, eight, wide = got.shape
    width = wide - 128
    whole = pl.BlockSpec(memory_space=pltpu.VMEM)
    return pl.pallas_call(
        functools.partial(pick_kernel, local_blocks),
        in_specs=[pl.BlockSpec(memory_space=pltpu.SMEM), whole],
        out_specs=[whole, whole],
        out_shape=[
            jax.ShapeDtypeStruct((nrows, eight, width), BF),
            jax.ShapeDtypeStruct((STEPS, width), F32),
        ],
        name="pick",
    )(order, got)


def feature_kernel(*refs):
    pieces = refs[:8]
    e_ref, shift_ref, r_ref, f_ref, out_ref, w_ref, left_ref, all_ref = refs[8:]
    step = pl.program_id(0)
    width = w_ref.shape[2]
    scale = 1.0 / width**0.5

    @pl.when(step == 0)
    def _():
        for shift in range(4):
            for other in range(2):
                px, pc = offsets(shift, other)
                at = pl.multiple_of(px * 256 + pc * 128, 128)
                for s in range(STEPS):
                    part = pieces[shift * 2 + other][s * 16 : s * 16 + 16, :, :]
                    w_ref[s, pl.ds(at, 128), :] = part.reshape(128, width)

    spots = [
        (row, s, col)
        for row in range(0, e_ref.shape[0], 512)
        for s in range(STEPS)
        for col in range(0, width, 256)
    ]

    def angles(row, s, col):
        return jnp.dot(e_ref[row : row + 512, :], w_ref[s, :, col : col + 256], preferred_element_type=F32)

    ahead = [angles(*spot) for spot in spots[:1]]
    for index, (row, s, col) in enumerate(spots):
        if index + 1 < len(spots):
            ahead.append(angles(*spots[index + 1]))
        angle = ahead.pop(0) + shift_ref[s : s + 1, col : col + 256]
        f_ref[row : row + 512, s * width + col : s * width + col + 256] = cosine(angle, scale).astype(BF)
    lane = lax.axis_index("x") * 128
    upper, lower = split_two(r_ref[...].T)
    left = [upper, lower]
    for s in range(STEPS):
        left.append(f_ref[:, pl.ds(pl.multiple_of(s * width + lane, 128), 128)].T)
    rows = e_ref.shape[0]
    here = pl.multiple_of(step * rows, rows)
    left_ref[:, pl.ds(here, rows)] = jnp.concatenate(left, axis=0)
    all_ref[pl.ds(here, rows), :] = f_ref[...]

    @pl.when(step == pl.num_programs(0) - 1)
    def _():
        half = lax.axis_index("c")

        def products(n, count):
            right = all_ref[:, n * 256 : n * 256 + 256]
            part = jnp.dot(left_ref[:count, :], right, preferred_element_type=F32)
            cross = part[0:128] + part[128:256]
            out_ref[n * 8 : n * 8 + 8, 24:56, :] = cross.T.reshape(8, 32, 128)
            return part

        for n in range(4):

            @pl.when(half == n % 2)
            def _():
                part = products(n, 512)
                for group, row in ((0, 256), (2, 384)) if n < 2 else ((1, 384),):
                    for side in range(2):
                        block = part[row : row + 128, side * 128 : side * 128 + 128].reshape(16, 8, 128)
                        out_ref[side * 16 : side * 16 + 16, group * 8 : group * 8 + 8, :] = block

            @pl.when(half != n % 2)
            def _():
                products(n, 256)


def features(pieces, embeddings, shifts, residuals):
    total, depth = embeddings.shape
    width = shifts.shape[1]
    tile = 512
    whole = pl.BlockSpec(memory_space=pltpu.VMEM)
    return pl.pallas_call(
        feature_kernel,
        grid=(total // tile,),
        in_specs=[whole] * 8
        + [
            pl.BlockSpec((tile, depth), lambda i: (i, 0)),
            whole,
            pl.BlockSpec((tile, 128), lambda i: (i, 0)),
        ],
        out_specs=[pl.BlockSpec((tile, STEPS * width), lambda i: (i, 0)), whole],
        out_shape=[
            jax.ShapeDtypeStruct((total, STEPS * width), BF),
            jax.ShapeDtypeStruct((32, 56, 128), F32),
        ],
        scratch_shapes=[
            pltpu.VMEM((STEPS, depth, width), BF),
            pltpu.VMEM((512, total), BF),
            pltpu.VMEM((total, STEPS * width), BF),
        ],
        compiler_params=pltpu.CompilerParams(vmem_limit_bytes=52 << 20),
        name="features",
    )(*pieces, embeddings, shifts, residuals)


def times(upper, lower, values):
    high, low = split_two(values)
    both = jnp.dot(upper, jnp.concatenate([high, low], axis=1), preferred_element_type=F32)
    return both[:, :128] + both[:, 128:] + jnp.dot(lower, high, preferred_element_type=F32)


def folded(values):
    part = [values[row : row + 8] for row in range(0, values.shape[0], 8)]
    while len(part) > 1:
        part = [part[i] + part[i + 1] for i in range(0, len(part), 2)]
    return part[0]


def total(parts):
    while len(parts) > 1:
        parts = [parts[i] + parts[i + 1] for i in range(0, len(parts), 2)]
    return jnp.sum(parts[0], axis=0, keepdims=True)


def conjugate_gradients(upper_ref, lower_ref, x_ref, r_ref, p_ref, ap_ref, v_ref, parts_ref, ridge):
    n = r_ref.shape[0]
    bound = (TOLERANCE * ridge) ** 2
    bands = [slice(row, row + 128) for row in range(0, n, 128)]

    def direct(band, p):
        p_ref[band] = p
        high, low = split_two(p)
        parts_ref[band, :128] = high
        parts_ref[band, 128:] = low

    first = upper_ref[:, :128].astype(F32)
    signs = jnp.where(first[:, :1] >= 0.0, 1.0, -1.0)
    once = jnp.dot(upper_ref[...], jnp.broadcast_to(signs, (n, 128)).astype(BF), preferred_element_type=F32)
    twice = jnp.dot(upper_ref[...], once.astype(BF), preferred_element_type=F32)
    norm = total([folded(twice * twice)])
    along = total([folded(once * once)])
    top = ridge + jnp.where(along > 0.0, total([folded(once * twice)]) / along, 0.0)
    v_ref[...] = twice * jnp.where(norm > 0.0, lax.rsqrt(norm), 0.0)
    keep = jnp.minimum((ridge + first[:1, :1]) / top, 1.0)
    drop = 1.0 - keep

    def weighed(rr, vr):
        return jnp.maximum(rr - drop * vr * vr, keep * rr)

    def one(rz):
        both = jnp.dot(upper_ref[...], parts_ref[...], preferred_element_type=F32)
        rest = jnp.dot(lower_ref[...], parts_ref[:, :128], preferred_element_type=F32)
        p = p_ref[...]
        ap = both[:, :128] + both[:, 128:] + rest + ridge * p
        ap_ref[...] = ap
        curve = total([folded(p * ap)])
        alpha = jnp.where(curve > 0.0, rz / curve, 0.0)
        squares, shadows = [], []
        for band in bands:
            r = r_ref[band] - alpha * ap_ref[band]
            r_ref[band] = r
            squares.append(folded(r * r))
            shadows.append(folded(v_ref[band] * r))
        rr, vr = total(squares), total(shadows)
        new = weighed(rr, vr)
        beta = jnp.where(rz > 0.0, new / rz, 0.0)
        shadow = drop * vr
        for band in bands:
            p = p_ref[band]
            x_ref[band] += alpha * p
            direct(band, r_ref[band] - shadow * v_ref[band] + beta * p)
        return rr, new

    def open_still(state):
        return jnp.logical_and(state[0] < MAX_LOOPS, state[1] > 0.0)

    def body(state):
        rz = state[2]
        for _ in range(UNROLL):
            rr, rz = one(rz)
        size = total([folded(x_ref[band] * x_ref[band]) for band in bands])
        return state[0] + 1, jnp.max(rr - bound * size), rz

    rr = total([folded(r_ref[band] * r_ref[band]) for band in bands])
    vr = total([folded(v_ref[band] * r_ref[band]) for band in bands])
    shadow = drop * vr
    for band in bands:
        x_ref[band] = jnp.zeros_like(r_ref[band])
        direct(band, r_ref[band] - shadow * v_ref[band])
    lax.while_loop(open_still, body, (jnp.int32(0), jnp.float32(1.0), weighed(rr, vr)))


def solve_kernel(ridge, *refs):
    pieces = refs[:8]
    cross_ref, old_ref, f_hbm, r_hbm, coef_ref, out_ref, upper, lower, f_ref, r_ref, x_ref, res_ref, p_ref, ap_ref, v_ref, parts_ref, delta_ref, sems = refs[8:]
    loads = [
        pltpu.make_async_copy(f_hbm, f_ref, sems.at[0]),
        pltpu.make_async_copy(r_hbm, r_ref, sems.at[1]),
    ]
    for load in loads:
        load.start()
    for shift in range(4):
        for other in range(2):
            ref = pieces[shift * 2 + other]
            px, pc = offsets(shift, other)
            row = pl.multiple_of(px * 128, 128)
            for group in range(3):
                for side in range(2):
                    lanes = pl.ds(pl.multiple_of(pc * 256 + side * 128, 128), 128)
                    block = ref[side * 16 : side * 16 + 16, group * 8 : group * 8 + 8, :].reshape(128, 128)
                    high, low = split_two(block)
                    upper[group, pl.ds(row, 128), lanes] = high
                    lower[group, pl.ds(row, 128), lanes] = low
    n = upper.shape[1]
    per = 32 // STEPS
    work = (x_ref, res_ref, p_ref, ap_ref, v_ref, parts_ref)
    res_ref[...] = cross_ref[:per].reshape(n, 128) - ridge * old_ref[0]
    conjugate_gradients(upper.at[0], lower.at[0], *work, ridge)
    first = x_ref[...]
    coef_ref[0] = old_ref[0] + first
    res_ref[...] = cross_ref[per:].reshape(n, 128) - ridge * old_ref[1] - times(upper[2], lower[2], first)
    high_first, low_first = split_two(first)
    delta_ref[:n, :128] = high_first
    delta_ref[:n, 128:] = low_first
    conjugate_gradients(upper.at[1], lower.at[1], *work, ridge)
    second = x_ref[...]
    coef_ref[1] = old_ref[1] + second
    high, low = split_two(second)
    delta_ref[n:, :128] = high
    delta_ref[n:, 128:] = low
    delta = delta_ref[...]
    tile = 256
    for load in loads:
        load.wait()
    for row in range(0, f_ref.shape[0], tile):
        both = jnp.dot(f_ref[row : row + tile, :], delta, preferred_element_type=F32)
        out_ref[row : row + tile, :] = r_ref[row : row + tile, :] - both[:, :128] - both[:, 128:]


def solve(pieces, cross, old, feats, residuals, ridge):
    def full(array):
        return pl.BlockSpec(array.shape, lambda: (0,) * array.ndim)

    return pl.pallas_call(
        functools.partial(solve_kernel, ridge),
        in_specs=[full(piece) for piece in pieces]
        + [full(cross), full(old), pl.BlockSpec(memory_space=pl.ANY), pl.BlockSpec(memory_space=pl.ANY)],
        out_specs=[full(old), full(residuals)],
        out_shape=[
            jax.ShapeDtypeStruct(old.shape, F32),
            jax.ShapeDtypeStruct(residuals.shape, F32),
        ],
        scratch_shapes=[
            pltpu.VMEM((3, 512, 512), BF),
            pltpu.VMEM((3, 512, 512), BF),
            pltpu.VMEM(feats.shape, BF),
            pltpu.VMEM(residuals.shape, F32),
            pltpu.VMEM((512, 128), F32),
            pltpu.VMEM((512, 128), F32),
            pltpu.VMEM((512, 128), F32),
            pltpu.VMEM((512, 128), F32),
            pltpu.VMEM((512, 128), F32),
            pltpu.VMEM((512, 256), BF),
            pltpu.VMEM((1024, 256), BF),
            pltpu.SemaphoreType.DMA((2,)),
        ],
        compiler_params=pltpu.CompilerParams(vmem_limit_bytes=52 << 20),
        name="solve",
    )(*pieces, cross, old, feats, residuals)


def exchange(values, axes):
    return lax.all_to_all(values, axes, split_axis=0, concat_axis=0, tiled=True)


def gather(values, axes, count):
    return exchange(jnp.broadcast_to(values[None], (count,) + values.shape), axes)


def spread(values):
    nx, nc = lax.axis_size("x"), lax.axis_size("c")
    moved = [values]
    for shift in range(1, nx):
        moved.append(lax.ppermute(values, "x", [(i, (i + shift) % nx) for i in range(nx)]))
    pieces = []
    for value in moved:
        pieces += [value, lax.ppermute(value, "c", [(i, (i + 1) % nc) for i in range(nc)])]
    return pieces


def body(embeddings, residuals, projections, phases, old_coef, block_order):
    local_blocks, depth, width = projections.shape
    nrows = lax.axis_size("z") * lax.axis_size("y")
    ridge = 0.25 * (embeddings.shape[0] * nrows) / width

    got = exchange(payload(block_order, projections, phases, nrows), ROWS)
    copies, shifts = pick(block_order, got, local_blocks)
    weights = spread(exchange(copies, ROWS))
    feats, parts = features(weights, embeddings, shifts, residuals)

    summed = jnp.sum(exchange(parts, ROWS), axis=0)
    grams = gather(summed[:24], ROWS, nrows)
    cross, grams = lax.optimization_barrier((summed[24:], grams))
    pieces = spread(grams)
    cross = gather(cross, ROWS, nrows)
    coef, current = solve(pieces, cross, old_coef, feats, residuals, ridge)
    return current, coef


def solution(mesh):
    grid = Mesh(mesh.devices.reshape(8, 4, 4, 2), ROWS + CLS)
    in_specs = (
        P(ROWS, None),
        P(ROWS, CLS),
        P(ROWS, None, None),
        P(ROWS, None),
        P(None, None, CLS),
        P(),
    )
    out_specs = (P(ROWS, CLS), P(None, None, CLS))
    return jax.shard_map(body, mesh=grid, in_specs=in_specs, out_specs=out_specs, check_vma=False)
```

```python
import functools
import math

import jax
import jax.numpy as jnp
from jax import lax
from jax.experimental import pallas as pl
from jax.experimental.pallas import tpu as pltpu
from jax.sharding import Mesh
from jax.sharding import PartitionSpec as P


STEPS = 2
BF = jnp.bfloat16
F32 = jnp.float32
ROWS = ("z", "y")
CLS = ("x", "c")

SINE = (6.28316404416301, -41.33714234877015, 81.3407680297695, -70.99342411797343)
TOLERANCE = 5e-5
MAX_LOOPS = 2000
UNROLL = 2


def cosine(angle, scale):
    turns = angle * (1.0 / (2.0 * math.pi))
    offset = turns - lax.round(turns, lax.RoundingMethod.TO_NEAREST_EVEN)
    q = 0.25 - jnp.abs(offset)
    z = q * q
    total = SINE[-1] * scale
    for coefficient in SINE[-2::-1]:
        total = total * z + coefficient * scale
    return total * q


def split_two(values):
    upper = values.astype(BF)
    return upper, (values - upper.astype(F32)).astype(BF)


def offsets(shift, other):
    return lax.rem(lax.axis_index("x") + 4 - shift, 4), lax.rem(lax.axis_index("c") + other, 2)


def payload_kernel(local_blocks, order, proj_ref, phase_ref, out_ref):
    part = 128
    width = proj_ref.shape[2]
    share = out_ref.shape[0] // STEPS
    at = pl.multiple_of((lax.axis_index("x") * 2 + lax.axis_index("c")) * part, part)
    for s in range(STEPS):
        slot = lax.rem(order[s], local_blocks)
        mine = proj_ref[pl.ds(slot, 1), pl.ds(at, part), :]
        out_ref[s * share : (s + 1) * share, :, :width] = mine.reshape(share, part // share, width)
    bands = []
    for s in range(STEPS):
        slot = lax.rem(order[s], local_blocks)
        shift = phase_ref[0:1, :].astype(F32)
        for k in range(1, phase_ref.shape[0]):
            shift = jnp.where(slot == k, phase_ref[k : k + 1, :].astype(F32), shift)
        bands += [shift[:, q * 128 : (q + 1) * 128] for q in range(width // 128)]
    band = jnp.concatenate(bands, axis=0).astype(BF)
    out_ref[:, :, width:] = jnp.broadcast_to(band[None], (out_ref.shape[0],) + band.shape)


def payload(order, projections, phases, nrows):
    local_blocks, _, width = projections.shape
    whole = pl.BlockSpec(memory_space=pltpu.VMEM)
    return pl.pallas_call(
        functools.partial(payload_kernel, local_blocks),
        in_specs=[pl.BlockSpec(memory_space=pltpu.SMEM), whole, whole],
        out_specs=whole,
        out_shape=jax.ShapeDtypeStruct((nrows, 8, width + 128), BF),
        name="payload",
    )(order, projections, phases)


def pick_kernel(local_blocks, order, got_ref, piece_ref, shift_ref):
    nrows, _, width = piece_ref.shape
    row = lax.axis_index("z") * 4 + lax.axis_index("y")
    source = jnp.where(row < nrows // STEPS, order[0], order[1]) // local_blocks
    piece = got_ref[pl.ds(source, 1), :, :width]
    piece_ref[...] = jnp.broadcast_to(piece, piece_ref.shape)
    for s in range(STEPS):
        band = got_ref[pl.ds(order[s] // local_blocks, 1), :, width:][0].astype(F32)
        for q in range(width // 128):
            row = s * (width // 128) + q
            shift_ref[s : s + 1, q * 128 : (q + 1) * 128] = band[row : row + 1, :]


def pick(order, got, local_blocks):
    nrows, eight, wide = got.shape
    width = wide - 128
    whole = pl.BlockSpec(memory_space=pltpu.VMEM)
    return pl.pallas_call(
        functools.partial(pick_kernel, local_blocks),
        in_specs=[pl.BlockSpec(memory_space=pltpu.SMEM), whole],
        out_specs=[whole, whole],
        out_shape=[
            jax.ShapeDtypeStruct((nrows, eight, width), BF),
            jax.ShapeDtypeStruct((STEPS, width), F32),
        ],
        name="pick",
    )(order, got)


def feature_kernel(*refs):
    pieces = refs[:8]
    e_ref, shift_ref, r_ref, f_ref, out_ref, w_ref, left_ref, all_ref = refs[8:]
    step = pl.program_id(0)
    width = w_ref.shape[2]
    scale = 1.0 / width**0.5

    @pl.when(step == 0)
    def _():
        for shift in range(4):
            for other in range(2):
                px, pc = offsets(shift, other)
                at = pl.multiple_of(px * 256 + pc * 128, 128)
                for s in range(STEPS):
                    part = pieces[shift * 2 + other][s * 16 : s * 16 + 16, :, :]
                    w_ref[s, pl.ds(at, 128), :] = part.reshape(128, width)

    spots = [
        (row, s, col)
        for row in range(0, e_ref.shape[0], 512)
        for s in range(STEPS)
        for col in range(0, width, 256)
    ]

    def angles(row, s, col):
        return jnp.dot(e_ref[row : row + 512, :], w_ref[s, :, col : col + 256], preferred_element_type=F32)

    ahead = [angles(*spot) for spot in spots[:1]]
    for index, (row, s, col) in enumerate(spots):
        if index + 1 < len(spots):
            ahead.append(angles(*spots[index + 1]))
        angle = ahead.pop(0) + shift_ref[s : s + 1, col : col + 256]
        f_ref[row : row + 512, s * width + col : s * width + col + 256] = cosine(angle, scale).astype(BF)
    lane = lax.axis_index("x") * 128
    upper, lower = split_two(r_ref[...].T)
    left = [upper, lower]
    for s in range(STEPS):
        left.append(f_ref[:, pl.ds(pl.multiple_of(s * width + lane, 128), 128)].T)
    rows = e_ref.shape[0]
    here = pl.multiple_of(step * rows, rows)
    left_ref[:, pl.ds(here, rows)] = jnp.concatenate(left, axis=0)
    all_ref[pl.ds(here, rows), :] = f_ref[...]

    @pl.when(step == pl.num_programs(0) - 1)
    def _():
        half = lax.axis_index("c")

        def products(n, count):
            right = all_ref[:, n * 256 : n * 256 + 256]
            part = jnp.dot(left_ref[:count, :], right, preferred_element_type=F32)
            cross = part[0:128] + part[128:256]
            out_ref[n * 8 : n * 8 + 8, 24:56, :] = cross.T.reshape(8, 32, 128)
            return part

        for n in range(4):

            @pl.when(half == n % 2)
            def _():
                part = products(n, 512)
                for group, row in ((0, 256), (2, 384)) if n < 2 else ((1, 384),):
                    for side in range(2):
                        block = part[row : row + 128, side * 128 : side * 128 + 128].reshape(16, 8, 128)
                        out_ref[side * 16 : side * 16 + 16, group * 8 : group * 8 + 8, :] = block

            @pl.when(half != n % 2)
            def _():
                products(n, 256)


def features(pieces, embeddings, shifts, residuals):
    total, depth = embeddings.shape
    width = shifts.shape[1]
    tile = 512
    whole = pl.BlockSpec(memory_space=pltpu.VMEM)
    return pl.pallas_call(
        feature_kernel,
        grid=(total // tile,),
        in_specs=[whole] * 8
        + [
            pl.BlockSpec((tile, depth), lambda i: (i, 0)),
            whole,
            pl.BlockSpec((tile, 128), lambda i: (i, 0)),
        ],
        out_specs=[pl.BlockSpec((tile, STEPS * width), lambda i: (i, 0)), whole],
        out_shape=[
            jax.ShapeDtypeStruct((total, STEPS * width), BF),
            jax.ShapeDtypeStruct((32, 56, 128), F32),
        ],
        scratch_shapes=[
            pltpu.VMEM((STEPS, depth, width), BF),
            pltpu.VMEM((512, total), BF),
            pltpu.VMEM((total, STEPS * width), BF),
        ],
        compiler_params=pltpu.CompilerParams(vmem_limit_bytes=52 << 20),
        name="features",
    )(*pieces, embeddings, shifts, residuals)


def times(upper, lower, values):
    high, low = split_two(values)
    both = jnp.dot(upper, jnp.concatenate([high, low], axis=1), preferred_element_type=F32)
    return both[:, :128] + both[:, 128:] + jnp.dot(lower, high, preferred_element_type=F32)


def folded(values):
    part = [values[row : row + 8] for row in range(0, values.shape[0], 8)]
    while len(part) > 1:
        part = [part[i] + part[i + 1] for i in range(0, len(part), 2)]
    return part[0]


def total(parts):
    while len(parts) > 1:
        parts = [parts[i] + parts[i + 1] for i in range(0, len(parts), 2)]
    return jnp.sum(parts[0], axis=0, keepdims=True)


def conjugate_gradients(upper_ref, lower_ref, x_ref, r_ref, p_ref, ap_ref, v_ref, parts_ref, ridge):
    n = r_ref.shape[0]
    bound = (TOLERANCE * ridge) ** 2
    bands = [slice(row, row + 128) for row in range(0, n, 128)]

    def direct(band, p):
        p_ref[band] = p
        high, low = split_two(p)
        parts_ref[band, :128] = high
        parts_ref[band, 128:] = low

    first = upper_ref[:, :128].astype(F32)
    signs = jnp.where(first[:, :1] >= 0.0, 1.0, -1.0)
    once = jnp.dot(upper_ref[...], jnp.broadcast_to(signs, (n, 128)).astype(BF), preferred_element_type=F32)
    twice = jnp.dot(upper_ref[...], once.astype(BF), preferred_element_type=F32)
    norm = total([folded(twice * twice)])
    along = total([folded(once * once)])
    top = ridge + jnp.where(along > 0.0, total([folded(once * twice)]) / along, 0.0)
    v_ref[...] = twice * jnp.where(norm > 0.0, lax.rsqrt(norm), 0.0)
    keep = jnp.minimum((ridge + first[:1, :1]) / top, 1.0)
    drop = 1.0 - keep

    def weighed(rr, vr):
        return jnp.maximum(rr - drop * vr * vr, keep * rr)

    def one(rz):
        both = jnp.dot(upper_ref[...], parts_ref[...], preferred_element_type=F32)
        rest = jnp.dot(lower_ref[...], parts_ref[:, :128], preferred_element_type=F32)
        p = p_ref[...]
        ap = both[:, :128] + both[:, 128:] + rest + ridge * p
        ap_ref[...] = ap
        curve = total([folded(p * ap)])
        alpha = jnp.where(curve > 0.0, rz / curve, 0.0)
        squares, shadows = [], []
        for band in bands:
            r = r_ref[band] - alpha * ap_ref[band]
            r_ref[band] = r
            squares.append(folded(r * r))
            shadows.append(folded(v_ref[band] * r))
        rr, vr = total(squares), total(shadows)
        new = weighed(rr, vr)
        beta = jnp.where(rz > 0.0, new / rz, 0.0)
        shadow = drop * vr
        for band in bands:
            p = p_ref[band]
            x_ref[band] += alpha * p
            direct(band, r_ref[band] - shadow * v_ref[band] + beta * p)
        return rr, new

    def open_still(state):
        return jnp.logical_and(state[0] < MAX_LOOPS, state[1] > 0.0)

    def body(state):
        rz = state[2]
        for _ in range(UNROLL):
            rr, rz = one(rz)
        size = total([folded(x_ref[band] * x_ref[band]) for band in bands])
        return state[0] + 1, jnp.max(rr - bound * size), rz

    rr = total([folded(r_ref[band] * r_ref[band]) for band in bands])
    vr = total([folded(v_ref[band] * r_ref[band]) for band in bands])
    shadow = drop * vr
    for band in bands:
        x_ref[band] = jnp.zeros_like(r_ref[band])
        direct(band, r_ref[band] - shadow * v_ref[band])
    lax.while_loop(open_still, body, (jnp.int32(0), jnp.float32(1.0), weighed(rr, vr)))


def solve_kernel(ridge, *refs):
    pieces = refs[:8]
    cross_ref, old_ref, f_hbm, r_hbm, coef_ref, out_ref, upper, lower, f_ref, r_ref, x_ref, res_ref, p_ref, ap_ref, v_ref, parts_ref, delta_ref, sems = refs[8:]
    loads = [
        pltpu.make_async_copy(f_hbm, f_ref, sems.at[0]),
        pltpu.make_async_copy(r_hbm, r_ref, sems.at[1]),
    ]
    for load in loads:
        load.start()
    for shift in range(4):
        for other in range(2):
            ref = pieces[shift * 2 + other]
            px, pc = offsets(shift, other)
            row = pl.multiple_of(px * 128, 128)
            for group in range(3):
                for side in range(2):
                    lanes = pl.ds(pl.multiple_of(pc * 256 + side * 128, 128), 128)
                    block = ref[side * 16 : side * 16 + 16, group * 8 : group * 8 + 8, :].reshape(128, 128)
                    high, low = split_two(block)
                    upper[group, pl.ds(row, 128), lanes] = high
                    lower[group, pl.ds(row, 128), lanes] = low
    n = upper.shape[1]
    per = 32 // STEPS
    work = (x_ref, res_ref, p_ref, ap_ref, v_ref, parts_ref)
    res_ref[...] = cross_ref[:per].reshape(n, 128) - ridge * old_ref[0]
    conjugate_gradients(upper.at[0], lower.at[0], *work, ridge)
    first = x_ref[...]
    coef_ref[0] = old_ref[0] + first
    res_ref[...] = cross_ref[per:].reshape(n, 128) - ridge * old_ref[1] - times(upper[2], lower[2], first)
    high_first, low_first = split_two(first)
    delta_ref[:n, :128] = high_first
    delta_ref[:n, 128:] = low_first
    conjugate_gradients(upper.at[1], lower.at[1], *work, ridge)
    second = x_ref[...]
    coef_ref[1] = old_ref[1] + second
    high, low = split_two(second)
    delta_ref[n:, :128] = high
    delta_ref[n:, 128:] = low
    delta = delta_ref[...]
    tile = 256
    for load in loads:
        load.wait()
    for row in range(0, f_ref.shape[0], tile):
        both = jnp.dot(f_ref[row : row + tile, :], delta, preferred_element_type=F32)
        out_ref[row : row + tile, :] = r_ref[row : row + tile, :] - both[:, :128] - both[:, 128:]


def solve(pieces, cross, old, feats, residuals, ridge):
    def full(array):
        return pl.BlockSpec(array.shape, lambda: (0,) * array.ndim)

    return pl.pallas_call(
        functools.partial(solve_kernel, ridge),
        in_specs=[full(piece) for piece in pieces]
        + [full(cross), full(old), pl.BlockSpec(memory_space=pl.ANY), pl.BlockSpec(memory_space=pl.ANY)],
        out_specs=[full(old), full(residuals)],
        out_shape=[
            jax.ShapeDtypeStruct(old.shape, F32),
            jax.ShapeDtypeStruct(residuals.shape, F32),
        ],
        scratch_shapes=[
            pltpu.VMEM((3, 512, 512), BF),
            pltpu.VMEM((3, 512, 512), BF),
            pltpu.VMEM(feats.shape, BF),
            pltpu.VMEM(residuals.shape, F32),
            pltpu.VMEM((512, 128), F32),
            pltpu.VMEM((512, 128), F32),
            pltpu.VMEM((512, 128), F32),
            pltpu.VMEM((512, 128), F32),
            pltpu.VMEM((512, 128), F32),
            pltpu.VMEM((512, 256), BF),
            pltpu.VMEM((1024, 256), BF),
            pltpu.SemaphoreType.DMA((2,)),
        ],
        compiler_params=pltpu.CompilerParams(vmem_limit_bytes=52 << 20),
        name="solve",
    )(*pieces, cross, old, feats, residuals)


def copies_kernel(got_ref, gram_ref, cross_ref):
    summed = [got_ref[i] for i in range(got_ref.shape[0])]
    while len(summed) > 1:
        summed = [summed[i] + summed[i + 1] for i in range(0, len(summed), 2)]
    first = gram_ref.shape[1]
    gram_ref[...] = jnp.broadcast_to(summed[0][None, :first], gram_ref.shape)
    cross_ref[...] = jnp.broadcast_to(summed[0][None, first:], cross_ref.shape)


def copies_of_sum(got):
    whole = pl.BlockSpec(memory_space=pltpu.VMEM)
    return pl.pallas_call(
        copies_kernel,
        in_specs=[whole],
        out_specs=[whole, whole],
        out_shape=[
            jax.ShapeDtypeStruct((got.shape[0], 24, 128), F32),
            jax.ShapeDtypeStruct((got.shape[0], 32, 128), F32),
        ],
        name="copies",
    )(got)


def exchange(values, axes):
    return lax.all_to_all(values, axes, split_axis=0, concat_axis=0, tiled=True)


def spread(values):
    nx, nc = lax.axis_size("x"), lax.axis_size("c")
    moved = [values]
    for shift in range(1, nx):
        moved.append(lax.ppermute(values, "x", [(i, (i + shift) % nx) for i in range(nx)]))
    pieces = []
    for value in moved:
        pieces += [value, lax.ppermute(value, "c", [(i, (i + 1) % nc) for i in range(nc)])]
    return pieces


def body(embeddings, residuals, projections, phases, old_coef, block_order):
    local_blocks, _, width = projections.shape
    nrows = lax.axis_size("z") * lax.axis_size("y")
    ridge = 0.25 * (embeddings.shape[0] * nrows) / width

    got = exchange(payload(block_order, projections, phases, nrows), ROWS)
    copies, shifts = pick(block_order, got, local_blocks)
    weights = spread(exchange(copies, ROWS))
    feats, parts = features(weights, embeddings, shifts, residuals)

    gram_copies, cross_copies = copies_of_sum(exchange(parts, ROWS))
    grams = exchange(gram_copies, ROWS)
    cross_copies, grams = lax.optimization_barrier((cross_copies, grams))
    pieces = spread(grams)
    cross = exchange(cross_copies, ROWS)
    coef, current = solve(pieces, cross, old_coef, feats, residuals, ridge)
    return current, coef


def solution(mesh):
    grid = Mesh(mesh.devices.reshape(8, 4, 4, 2), ROWS + CLS)
    in_specs = (
        P(ROWS, None),
        P(ROWS, CLS),
        P(ROWS, None, None),
        P(ROWS, None),
        P(None, None, CLS),
        P(),
    )
    out_specs = (P(ROWS, CLS), P(None, None, CLS))
    return jax.shard_map(body, mesh=grid, in_specs=in_specs, out_specs=out_specs, check_vma=False)
```

```python
import functools
import math

import jax
import jax.numpy as jnp
from jax import lax
from jax.experimental import pallas as pl
from jax.experimental.pallas import tpu as pltpu
from jax.sharding import Mesh
from jax.sharding import PartitionSpec as P


STEPS = 2
BF = jnp.bfloat16
F32 = jnp.float32
ROWS = ("z", "y")
CLS = ("x", "c")

SINE = (6.28316404416301, -41.33714234877015, 81.3407680297695, -70.99342411797343)
TOLERANCE = 5e-5
MAX_LOOPS = 2000
UNROLL = 2


def cosine(angle, scale):
    turns = angle * (1.0 / (2.0 * math.pi))
    offset = turns - lax.round(turns, lax.RoundingMethod.TO_NEAREST_EVEN)
    q = 0.25 - jnp.abs(offset)
    z = q * q
    total = SINE[-1] * scale
    for coefficient in SINE[-2::-1]:
        total = total * z + coefficient * scale
    return total * q


def split_two(values):
    upper = values.astype(BF)
    return upper, (values - upper.astype(F32)).astype(BF)


def offsets(shift, other):
    return lax.rem(lax.axis_index("x") + 4 - shift, 4), lax.rem(lax.axis_index("c") + other, 2)


def payload_kernel(local_blocks, order, proj_hbm, phase_ref, out_ref, slice_ref, sems):
    part = slice_ref.shape[1]
    width = slice_ref.shape[2]
    share = out_ref.shape[0] // STEPS
    at = pl.multiple_of((lax.axis_index("x") * 2 + lax.axis_index("c")) * part, part)
    slots = [lax.rem(order[s], local_blocks) for s in range(STEPS)]
    loads = [
        pltpu.make_async_copy(proj_hbm.at[slots[s], pl.ds(at, part), :], slice_ref.at[s], sems.at[s])
        for s in range(STEPS)
    ]
    for load in loads:
        load.start()
    bands = []
    for s in range(STEPS):
        shift = phase_ref[0:1, :].astype(F32)
        for k in range(1, phase_ref.shape[0]):
            shift = jnp.where(slots[s] == k, phase_ref[k : k + 1, :].astype(F32), shift)
        bands += [shift[:, q * 128 : (q + 1) * 128] for q in range(width // 128)]
    band = jnp.concatenate(bands, axis=0).astype(BF)
    out_ref[:, :, width:] = jnp.broadcast_to(band[None], (out_ref.shape[0],) + band.shape)
    for s in range(STEPS):
        loads[s].wait()
        out_ref[s * share : (s + 1) * share, :, :width] = slice_ref[s].reshape(share, part // share, width)


def payload(order, projections, phases, nrows):
    local_blocks, _, width = projections.shape
    whole = pl.BlockSpec(memory_space=pltpu.VMEM)
    return pl.pallas_call(
        functools.partial(payload_kernel, local_blocks),
        in_specs=[pl.BlockSpec(memory_space=pltpu.SMEM), pl.BlockSpec(memory_space=pl.ANY), whole],
        out_specs=whole,
        out_shape=jax.ShapeDtypeStruct((nrows, 8, width + 128), BF),
        scratch_shapes=[pltpu.VMEM((STEPS, 128, width), BF), pltpu.SemaphoreType.DMA((STEPS,))],
        name="payload",
    )(order, projections, phases)


def pick_kernel(local_blocks, order, got_ref, piece_ref, shift_ref):
    nrows, _, width = piece_ref.shape
    row = lax.axis_index("z") * 4 + lax.axis_index("y")
    source = jnp.where(row < nrows // STEPS, order[0], order[1]) // local_blocks
    piece = got_ref[pl.ds(source, 1), :, :width]
    piece_ref[...] = jnp.broadcast_to(piece, piece_ref.shape)
    for s in range(STEPS):
        band = got_ref[pl.ds(order[s] // local_blocks, 1), :, width:][0].astype(F32)
        for q in range(width // 128):
            row = s * (width // 128) + q
            shift_ref[s : s + 1, q * 128 : (q + 1) * 128] = band[row : row + 1, :]


def pick(order, got, local_blocks):
    nrows, eight, wide = got.shape
    width = wide - 128
    whole = pl.BlockSpec(memory_space=pltpu.VMEM)
    return pl.pallas_call(
        functools.partial(pick_kernel, local_blocks),
        in_specs=[pl.BlockSpec(memory_space=pltpu.SMEM), whole],
        out_specs=[whole, whole],
        out_shape=[
            jax.ShapeDtypeStruct((nrows, eight, width), BF),
            jax.ShapeDtypeStruct((STEPS, width), F32),
        ],
        name="pick",
    )(order, got)


def feature_kernel(*refs):
    pieces = refs[:8]
    e_ref, shift_ref, r_ref, f_ref, out_ref, w_ref, left_ref, all_ref = refs[8:]
    step = pl.program_id(0)
    width = w_ref.shape[2]
    scale = 1.0 / width**0.5

    @pl.when(step == 0)
    def _():
        for shift in range(4):
            for other in range(2):
                px, pc = offsets(shift, other)
                at = pl.multiple_of(px * 256 + pc * 128, 128)
                for s in range(STEPS):
                    part = pieces[shift * 2 + other][s * 16 : s * 16 + 16, :, :]
                    w_ref[s, pl.ds(at, 128), :] = part.reshape(128, width)

    spots = [
        (row, s, col)
        for row in range(0, e_ref.shape[0], 512)
        for s in range(STEPS)
        for col in range(0, width, 256)
    ]

    def angles(row, s, col):
        return jnp.dot(e_ref[row : row + 512, :], w_ref[s, :, col : col + 256], preferred_element_type=F32)

    ahead = [angles(*spot) for spot in spots[:1]]
    for index, (row, s, col) in enumerate(spots):
        if index + 1 < len(spots):
            ahead.append(angles(*spots[index + 1]))
        angle = ahead.pop(0) + shift_ref[s : s + 1, col : col + 256]
        f_ref[row : row + 512, s * width + col : s * width + col + 256] = cosine(angle, scale).astype(BF)
    lane = lax.axis_index("x") * 128
    upper, lower = split_two(r_ref[...].T)
    left = [upper, lower]
    for s in range(STEPS):
        left.append(f_ref[:, pl.ds(pl.multiple_of(s * width + lane, 128), 128)].T)
    rows = e_ref.shape[0]
    here = pl.multiple_of(step * rows, rows)
    left_ref[:, pl.ds(here, rows)] = jnp.concatenate(left, axis=0)
    all_ref[pl.ds(here, rows), :] = f_ref[...]

    @pl.when(step == pl.num_programs(0) - 1)
    def _():
        half = lax.axis_index("c")

        def products(n, count):
            right = all_ref[:, n * 256 : n * 256 + 256]
            part = jnp.dot(left_ref[:count, :], right, preferred_element_type=F32)
            cross = part[0:128] + part[128:256]
            out_ref[n * 8 : n * 8 + 8, 24:56, :] = cross.T.reshape(8, 32, 128)
            return part

        for n in range(4):

            @pl.when(half == n % 2)
            def _():
                part = products(n, 512)
                for group, row in ((0, 256), (2, 384)) if n < 2 else ((1, 384),):
                    for side in range(2):
                        block = part[row : row + 128, side * 128 : side * 128 + 128].reshape(16, 8, 128)
                        out_ref[side * 16 : side * 16 + 16, group * 8 : group * 8 + 8, :] = block

            @pl.when(half != n % 2)
            def _():
                products(n, 256)


def features(pieces, embeddings, shifts, residuals):
    total, depth = embeddings.shape
    width = shifts.shape[1]
    tile = 512
    whole = pl.BlockSpec(memory_space=pltpu.VMEM)
    return pl.pallas_call(
        feature_kernel,
        grid=(total // tile,),
        in_specs=[whole] * 8
        + [
            pl.BlockSpec((tile, depth), lambda i: (i, 0)),
            whole,
            pl.BlockSpec((tile, 128), lambda i: (i, 0)),
        ],
        out_specs=[pl.BlockSpec((tile, STEPS * width), lambda i: (i, 0)), whole],
        out_shape=[
            jax.ShapeDtypeStruct((total, STEPS * width), BF),
            jax.ShapeDtypeStruct((32, 56, 128), F32),
        ],
        scratch_shapes=[
            pltpu.VMEM((STEPS, depth, width), BF),
            pltpu.VMEM((512, total), BF),
            pltpu.VMEM((total, STEPS * width), BF),
        ],
        compiler_params=pltpu.CompilerParams(vmem_limit_bytes=52 << 20),
        name="features",
    )(*pieces, embeddings, shifts, residuals)


def times(upper, lower, values):
    high, low = split_two(values)
    both = jnp.dot(upper, jnp.concatenate([high, low], axis=1), preferred_element_type=F32)
    return both[:, :128] + both[:, 128:] + jnp.dot(lower, high, preferred_element_type=F32)


def folded(values):
    part = [values[row : row + 8] for row in range(0, values.shape[0], 8)]
    while len(part) > 1:
        part = [part[i] + part[i + 1] for i in range(0, len(part), 2)]
    return part[0]


def total(parts):
    while len(parts) > 1:
        parts = [parts[i] + parts[i + 1] for i in range(0, len(parts), 2)]
    return jnp.sum(parts[0], axis=0, keepdims=True)


def conjugate_gradients(upper_ref, lower_ref, x_ref, r_ref, p_ref, ap_ref, v_ref, parts_ref, ridge):
    n = r_ref.shape[0]
    bound = (TOLERANCE * ridge) ** 2
    bands = [slice(row, row + 128) for row in range(0, n, 128)]

    def direct(band, p):
        p_ref[band] = p
        high, low = split_two(p)
        parts_ref[band, :128] = high
        parts_ref[band, 128:] = low

    first = upper_ref[:, :128].astype(F32)
    signs = jnp.where(first[:, :1] >= 0.0, 1.0, -1.0)
    once = jnp.dot(upper_ref[...], jnp.broadcast_to(signs, (n, 128)).astype(BF), preferred_element_type=F32)
    twice = jnp.dot(upper_ref[...], once.astype(BF), preferred_element_type=F32)
    norm = total([folded(twice * twice)])
    along = total([folded(once * once)])
    top = ridge + jnp.where(along > 0.0, total([folded(once * twice)]) / along, 0.0)
    v_ref[...] = twice * jnp.where(norm > 0.0, lax.rsqrt(norm), 0.0)
    keep = jnp.minimum((ridge + first[:1, :1]) / top, 1.0)
    drop = 1.0 - keep

    def weighed(rr, vr):
        return jnp.maximum(rr - drop * vr * vr, keep * rr)

    def one(rz):
        both = jnp.dot(upper_ref[...], parts_ref[...], preferred_element_type=F32)
        rest = jnp.dot(lower_ref[...], parts_ref[:, :128], preferred_element_type=F32)
        p = p_ref[...]
        ap = both[:, :128] + both[:, 128:] + rest + ridge * p
        ap_ref[...] = ap
        curve = total([folded(p * ap)])
        alpha = jnp.where(curve > 0.0, rz / curve, 0.0)
        squares, shadows = [], []
        for band in bands:
            r = r_ref[band] - alpha * ap_ref[band]
            r_ref[band] = r
            squares.append(folded(r * r))
            shadows.append(folded(v_ref[band] * r))
        rr, vr = total(squares), total(shadows)
        new = weighed(rr, vr)
        beta = jnp.where(rz > 0.0, new / rz, 0.0)
        shadow = drop * vr
        for band in bands:
            p = p_ref[band]
            x_ref[band] += alpha * p
            direct(band, r_ref[band] - shadow * v_ref[band] + beta * p)
        return rr, new

    def open_still(state):
        return jnp.logical_and(state[0] < MAX_LOOPS, state[1] > 0.0)

    def body(state):
        rz = state[2]
        for _ in range(UNROLL):
            rr, rz = one(rz)
        size = total([folded(x_ref[band] * x_ref[band]) for band in bands])
        return state[0] + 1, jnp.max(rr - bound * size), rz

    rr = total([folded(r_ref[band] * r_ref[band]) for band in bands])
    vr = total([folded(v_ref[band] * r_ref[band]) for band in bands])
    shadow = drop * vr
    for band in bands:
        x_ref[band] = jnp.zeros_like(r_ref[band])
        direct(band, r_ref[band] - shadow * v_ref[band])
    lax.while_loop(open_still, body, (jnp.int32(0), jnp.float32(1.0), weighed(rr, vr)))


def solve_kernel(ridge, *refs):
    pieces = refs[:8]
    cross_hbm, old_hbm, f_hbm, r_hbm, coef_ref, out_ref, pieces_ref, cross_ref, old_ref, upper, lower, f_ref, r_ref, x_ref, res_ref, p_ref, ap_ref, v_ref, parts_ref, delta_ref, sems = refs[8:]
    loads = [pltpu.make_async_copy(pieces[i], pieces_ref.at[i], sems.at[i]) for i in range(8)]
    rest = ((cross_hbm, cross_ref), (old_hbm, old_ref), (f_hbm, f_ref), (r_hbm, r_ref))
    loads += [pltpu.make_async_copy(there, here, sems.at[8 + i]) for i, (there, here) in enumerate(rest)]
    for load in loads:
        load.start()
    for shift in range(4):
        for other in range(2):
            loads[shift * 2 + other].wait()
            ref = pieces_ref.at[shift * 2 + other]
            px, pc = offsets(shift, other)
            row = pl.multiple_of(px * 128, 128)
            for group in range(3):
                for side in range(2):
                    lanes = pl.ds(pl.multiple_of(pc * 256 + side * 128, 128), 128)
                    block = ref[side * 16 : side * 16 + 16, group * 8 : group * 8 + 8, :].reshape(128, 128)
                    high, low = split_two(block)
                    upper[group, pl.ds(row, 128), lanes] = high
                    lower[group, pl.ds(row, 128), lanes] = low
    n = upper.shape[1]
    per = 32 // STEPS
    work = (x_ref, res_ref, p_ref, ap_ref, v_ref, parts_ref)
    for load in loads[8:10]:
        load.wait()
    res_ref[...] = cross_ref[:per].reshape(n, 128) - ridge * old_ref[0]
    conjugate_gradients(upper.at[0], lower.at[0], *work, ridge)
    first = x_ref[...]
    coef_ref[0] = old_ref[0] + first
    res_ref[...] = cross_ref[per:].reshape(n, 128) - ridge * old_ref[1] - times(upper[2], lower[2], first)
    high_first, low_first = split_two(first)
    delta_ref[:n, :128] = high_first
    delta_ref[:n, 128:] = low_first
    conjugate_gradients(upper.at[1], lower.at[1], *work, ridge)
    second = x_ref[...]
    coef_ref[1] = old_ref[1] + second
    high, low = split_two(second)
    delta_ref[n:, :128] = high
    delta_ref[n:, 128:] = low
    delta = delta_ref[...]
    tile = 256
    for load in loads[10:]:
        load.wait()
    for row in range(0, f_ref.shape[0], tile):
        both = jnp.dot(f_ref[row : row + tile, :], delta, preferred_element_type=F32)
        out_ref[row : row + tile, :] = r_ref[row : row + tile, :] - both[:, :128] - both[:, 128:]


def solve(pieces, cross, old, feats, residuals, ridge):
    def full(array):
        return pl.BlockSpec(array.shape, lambda: (0,) * array.ndim)

    return pl.pallas_call(
        functools.partial(solve_kernel, ridge),
        in_specs=[pl.BlockSpec(memory_space=pl.ANY)] * 12,
        out_specs=[full(old), full(residuals)],
        out_shape=[
            jax.ShapeDtypeStruct(old.shape, F32),
            jax.ShapeDtypeStruct(residuals.shape, F32),
        ],
        scratch_shapes=[
            pltpu.VMEM((8, 32, 24, 128), F32),
            pltpu.VMEM(cross.shape, F32),
            pltpu.VMEM(old.shape, F32),
            pltpu.VMEM((3, 512, 512), BF),
            pltpu.VMEM((3, 512, 512), BF),
            pltpu.VMEM(feats.shape, BF),
            pltpu.VMEM(residuals.shape, F32),
            pltpu.VMEM((512, 128), F32),
            pltpu.VMEM((512, 128), F32),
            pltpu.VMEM((512, 128), F32),
            pltpu.VMEM((512, 128), F32),
            pltpu.VMEM((512, 128), F32),
            pltpu.VMEM((512, 256), BF),
            pltpu.VMEM((1024, 256), BF),
            pltpu.SemaphoreType.DMA((12,)),
        ],
        compiler_params=pltpu.CompilerParams(vmem_limit_bytes=52 << 20),
        name="solve",
    )(*pieces, cross, old, feats, residuals)


def copies_kernel(got_ref, gram_ref, cross_ref):
    summed = [got_ref[i] for i in range(got_ref.shape[0])]
    while len(summed) > 1:
        summed = [summed[i] + summed[i + 1] for i in range(0, len(summed), 2)]
    first = gram_ref.shape[1]
    gram_ref[...] = jnp.broadcast_to(summed[0][None, :first], gram_ref.shape)
    cross_ref[...] = jnp.broadcast_to(summed[0][None, first:], cross_ref.shape)


def copies_of_sum(got):
    whole = pl.BlockSpec(memory_space=pltpu.VMEM)
    return pl.pallas_call(
        copies_kernel,
        in_specs=[whole],
        out_specs=[whole, whole],
        out_shape=[
            jax.ShapeDtypeStruct((got.shape[0], 24, 128), F32),
            jax.ShapeDtypeStruct((got.shape[0], 32, 128), F32),
        ],
        name="copies",
    )(got)


def exchange(values, axes):
    return lax.all_to_all(values, axes, split_axis=0, concat_axis=0, tiled=True)


def spread(values):
    nx, nc = lax.axis_size("x"), lax.axis_size("c")
    moved = [values]
    for shift in range(1, nx):
        moved.append(lax.ppermute(values, "x", [(i, (i + shift) % nx) for i in range(nx)]))
    pieces = []
    for value in moved:
        pieces += [value, lax.ppermute(value, "c", [(i, (i + 1) % nc) for i in range(nc)])]
    return pieces


def body(embeddings, residuals, projections, phases, old_coef, block_order):
    local_blocks, _, width = projections.shape
    nrows = lax.axis_size("z") * lax.axis_size("y")
    ridge = 0.25 * (embeddings.shape[0] * nrows) / width

    got = exchange(payload(block_order, projections, phases, nrows), ROWS)
    copies, shifts = pick(block_order, got, local_blocks)
    weights = spread(exchange(copies, ROWS))
    feats, parts = features(weights, embeddings, shifts, residuals)

    gram_copies, cross_copies = copies_of_sum(exchange(parts, ROWS))
    grams = exchange(gram_copies, ROWS)
    cross_copies, grams = lax.optimization_barrier((cross_copies, grams))
    pieces = spread(grams)
    cross = exchange(cross_copies, ROWS)
    coef, current = solve(pieces, cross, old_coef, feats, residuals, ridge)
    return current, coef


def solution(mesh):
    grid = Mesh(mesh.devices.reshape(8, 4, 4, 2), ROWS + CLS)
    in_specs = (
        P(ROWS, None),
        P(ROWS, CLS),
        P(ROWS, None, None),
        P(ROWS, None),
        P(None, None, CLS),
        P(),
    )
    out_specs = (P(ROWS, CLS), P(None, None, CLS))
    return jax.shard_map(body, mesh=grid, in_specs=in_specs, out_specs=out_specs, check_vma=False)
```

```python
import functools
import math

import jax
import jax.numpy as jnp
from jax import lax
from jax.experimental import pallas as pl
from jax.experimental.pallas import tpu as pltpu
from jax.sharding import Mesh
from jax.sharding import PartitionSpec as P


STEPS = 2
BF = jnp.bfloat16
F32 = jnp.float32
ROWS = ("z", "y")
CLS = ("x", "c")

SINE = (6.28316404416301, -41.33714234877015, 81.3407680297695, -70.99342411797343)
TOLERANCE = 5e-5
MAX_LOOPS = 2000
UNROLL = 2


def cosine(angle, scale):
    turns = angle * (1.0 / (2.0 * math.pi))
    offset = turns - lax.round(turns, lax.RoundingMethod.TO_NEAREST_EVEN)
    q = 0.25 - jnp.abs(offset)
    z = q * q
    total = SINE[-1] * scale
    for coefficient in SINE[-2::-1]:
        total = total * z + coefficient * scale
    return total * q


def split_two(values):
    upper = values.astype(BF)
    return upper, (values - upper.astype(F32)).astype(BF)


def offsets(shift, other):
    return lax.rem(lax.axis_index("x") + 4 - shift, 4), lax.rem(lax.axis_index("c") + other, 2)


def payload_kernel(local_blocks, order, proj_hbm, phase_ref, out_ref, slice_ref, sems):
    part = slice_ref.shape[1]
    width = slice_ref.shape[2]
    share = out_ref.shape[0] // STEPS
    at = pl.multiple_of((lax.axis_index("x") * 2 + lax.axis_index("c")) * part, part)
    slots = [lax.rem(order[s], local_blocks) for s in range(STEPS)]
    loads = [
        pltpu.make_async_copy(proj_hbm.at[slots[s], pl.ds(at, part), :], slice_ref.at[s], sems.at[s])
        for s in range(STEPS)
    ]
    for load in loads:
        load.start()
    bands = []
    for s in range(STEPS):
        shift = phase_ref[0:1, :].astype(F32)
        for k in range(1, phase_ref.shape[0]):
            shift = jnp.where(slots[s] == k, phase_ref[k : k + 1, :].astype(F32), shift)
        bands += [shift[:, q * 128 : (q + 1) * 128] for q in range(width // 128)]
    band = jnp.concatenate(bands, axis=0).astype(BF)
    out_ref[:, :, width:] = jnp.broadcast_to(band[None], (out_ref.shape[0],) + band.shape)
    for s in range(STEPS):
        loads[s].wait()
        out_ref[s * share : (s + 1) * share, :, :width] = slice_ref[s].reshape(share, part // share, width)


def payload(order, projections, phases, nrows):
    local_blocks, _, width = projections.shape
    whole = pl.BlockSpec(memory_space=pltpu.VMEM)
    return pl.pallas_call(
        functools.partial(payload_kernel, local_blocks),
        in_specs=[pl.BlockSpec(memory_space=pltpu.SMEM), pl.BlockSpec(memory_space=pl.ANY), whole],
        out_specs=whole,
        out_shape=jax.ShapeDtypeStruct((nrows, 8, width + 128), BF),
        scratch_shapes=[pltpu.VMEM((STEPS, 128, width), BF), pltpu.SemaphoreType.DMA((STEPS,))],
        name="payload",
    )(order, projections, phases)


def pick_kernel(local_blocks, order, got_ref, piece_ref, shift_ref):
    nrows, _, width = piece_ref.shape
    row = lax.axis_index("z") * 4 + lax.axis_index("y")
    source = jnp.where(row < nrows // STEPS, order[0], order[1]) // local_blocks
    piece = got_ref[pl.ds(source, 1), :, :width]
    piece_ref[...] = jnp.broadcast_to(piece, piece_ref.shape)
    for s in range(STEPS):
        band = got_ref[pl.ds(order[s] // local_blocks, 1), :, width:][0].astype(F32)
        for q in range(width // 128):
            row = s * (width // 128) + q
            shift_ref[s : s + 1, q * 128 : (q + 1) * 128] = band[row : row + 1, :]


def pick(order, got, local_blocks):
    nrows, eight, wide = got.shape
    width = wide - 128
    whole = pl.BlockSpec(memory_space=pltpu.VMEM)
    return pl.pallas_call(
        functools.partial(pick_kernel, local_blocks),
        in_specs=[pl.BlockSpec(memory_space=pltpu.SMEM), whole],
        out_specs=[whole, whole],
        out_shape=[
            jax.ShapeDtypeStruct((nrows, eight, width), BF),
            jax.ShapeDtypeStruct((STEPS, width), F32),
        ],
        name="pick",
    )(order, got)


def feature_kernel(*refs):
    pieces = refs[:8]
    e_ref, shift_ref, r_ref, f_ref, out_ref, w_ref, left_ref, all_ref = refs[8:]
    step = pl.program_id(0)
    width = w_ref.shape[2]
    scale = 1.0 / width**0.5

    @pl.when(step == 0)
    def _():
        for shift in range(4):
            for other in range(2):
                px, pc = offsets(shift, other)
                at = pl.multiple_of(px * 256 + pc * 128, 128)
                for s in range(STEPS):
                    part = pieces[shift * 2 + other][s * 16 : s * 16 + 16, :, :]
                    w_ref[s, pl.ds(at, 128), :] = part.reshape(128, width)

    spots = [
        (row, s, col)
        for row in range(0, e_ref.shape[0], 512)
        for s in range(STEPS)
        for col in range(0, width, 256)
    ]

    def angles(row, s, col):
        return jnp.dot(e_ref[row : row + 512, :], w_ref[s, :, col : col + 256], preferred_element_type=F32)

    ahead = [angles(*spot) for spot in spots[:1]]
    for index, (row, s, col) in enumerate(spots):
        if index + 1 < len(spots):
            ahead.append(angles(*spots[index + 1]))
        angle = ahead.pop(0) + shift_ref[s : s + 1, col : col + 256]
        f_ref[row : row + 512, s * width + col : s * width + col + 256] = cosine(angle, scale).astype(BF)
    lane = lax.axis_index("x") * 128
    upper, lower = split_two(r_ref[...].T)
    left = [upper, lower]
    for s in range(STEPS):
        left.append(f_ref[:, pl.ds(pl.multiple_of(s * width + lane, 128), 128)].T)
    rows = e_ref.shape[0]
    here = pl.multiple_of(step * rows, rows)
    left_ref[:, pl.ds(here, rows)] = jnp.concatenate(left, axis=0)
    all_ref[pl.ds(here, rows), :] = f_ref[...]

    @pl.when(step == pl.num_programs(0) - 1)
    def _():
        half = lax.axis_index("c")

        def products(n, count):
            right = all_ref[:, n * 256 : n * 256 + 256]
            part = jnp.dot(left_ref[:count, :], right, preferred_element_type=F32)
            cross = part[0:128] + part[128:256]
            out_ref[n * 8 : n * 8 + 8, 24:56, :] = cross.T.reshape(8, 32, 128)
            return part

        for n in range(4):

            @pl.when(half == n % 2)
            def _():
                part = products(n, 512)
                for group, row in ((0, 256), (2, 384)) if n < 2 else ((1, 384),):
                    for side in range(2):
                        block = part[row : row + 128, side * 128 : side * 128 + 128].reshape(16, 8, 128)
                        out_ref[side * 16 : side * 16 + 16, group * 8 : group * 8 + 8, :] = block

            @pl.when(half != n % 2)
            def _():
                products(n, 256)


def features(pieces, embeddings, shifts, residuals):
    total, depth = embeddings.shape
    width = shifts.shape[1]
    tile = 512
    whole = pl.BlockSpec(memory_space=pltpu.VMEM)
    return pl.pallas_call(
        feature_kernel,
        grid=(total // tile,),
        in_specs=[whole] * 8
        + [
            pl.BlockSpec((tile, depth), lambda i: (i, 0)),
            pl.BlockSpec((STEPS, width), lambda i: (0, 0)),
            pl.BlockSpec((tile, 128), lambda i: (i, 0)),
        ],
        out_specs=[pl.BlockSpec((tile, STEPS * width), lambda i: (i, 0)), whole],
        out_shape=[
            jax.ShapeDtypeStruct((total, STEPS * width), BF),
            jax.ShapeDtypeStruct((32, 56, 128), F32),
        ],
        scratch_shapes=[
            pltpu.VMEM((STEPS, depth, width), BF),
            pltpu.VMEM((512, total), BF),
            pltpu.VMEM((total, STEPS * width), BF),
        ],
        compiler_params=pltpu.CompilerParams(vmem_limit_bytes=48 << 20),
        name="features",
    )(*pieces, embeddings, shifts, residuals)


def times(upper, lower, values):
    high, low = split_two(values)
    both = jnp.dot(upper, jnp.concatenate([high, low], axis=1), preferred_element_type=F32)
    return both[:, :128] + both[:, 128:] + jnp.dot(lower, high, preferred_element_type=F32)


def folded(values):
    part = [values[row : row + 8] for row in range(0, values.shape[0], 8)]
    while len(part) > 1:
        part = [part[i] + part[i + 1] for i in range(0, len(part), 2)]
    return part[0]


def total(parts):
    while len(parts) > 1:
        parts = [parts[i] + parts[i + 1] for i in range(0, len(parts), 2)]
    return jnp.sum(parts[0], axis=0, keepdims=True)


def conjugate_gradients(upper_ref, lower_ref, x_ref, r_ref, p_ref, ap_ref, v_ref, parts_ref, ridge):
    n = r_ref.shape[0]
    bound = (TOLERANCE * ridge) ** 2
    bands = [slice(row, row + 128) for row in range(0, n, 128)]

    def direct(band, p):
        p_ref[band] = p
        high, low = split_two(p)
        parts_ref[band, :128] = high
        parts_ref[band, 128:] = low

    first = upper_ref[:, :128].astype(F32)
    signs = jnp.where(first[:, :1] >= 0.0, 1.0, -1.0)
    once = jnp.dot(upper_ref[...], jnp.broadcast_to(signs, (n, 128)).astype(BF), preferred_element_type=F32)
    twice = jnp.dot(upper_ref[...], once.astype(BF), preferred_element_type=F32)
    norm = total([folded(twice * twice)])
    along = total([folded(once * once)])
    top = ridge + jnp.where(along > 0.0, total([folded(once * twice)]) / along, 0.0)
    v_ref[...] = twice * jnp.where(norm > 0.0, lax.rsqrt(norm), 0.0)
    keep = jnp.minimum((ridge + first[:1, :1]) / top, 1.0)
    drop = 1.0 - keep

    def weighed(rr, vr):
        return jnp.maximum(rr - drop * vr * vr, keep * rr)

    def one(rz):
        both = jnp.dot(upper_ref[...], parts_ref[...], preferred_element_type=F32)
        rest = jnp.dot(lower_ref[...], parts_ref[:, :128], preferred_element_type=F32)
        p = p_ref[...]
        ap = both[:, :128] + both[:, 128:] + rest + ridge * p
        ap_ref[...] = ap
        curve = total([folded(p * ap)])
        alpha = jnp.where(curve > 0.0, rz / curve, 0.0)
        squares, shadows = [], []
        for band in bands:
            r = r_ref[band] - alpha * ap_ref[band]
            r_ref[band] = r
            squares.append(folded(r * r))
            shadows.append(folded(v_ref[band] * r))
        rr, vr = total(squares), total(shadows)
        new = weighed(rr, vr)
        beta = jnp.where(rz > 0.0, new / rz, 0.0)
        shadow = drop * vr
        for band in bands:
            p = p_ref[band]
            x_ref[band] += alpha * p
            direct(band, r_ref[band] - shadow * v_ref[band] + beta * p)
        return rr, new

    def open_still(state):
        return jnp.logical_and(state[0] < MAX_LOOPS, state[1] > 0.0)

    def body(state):
        rz = state[2]
        for _ in range(UNROLL):
            rr, rz = one(rz)
        size = total([folded(x_ref[band] * x_ref[band]) for band in bands])
        return state[0] + 1, jnp.max(rr - bound * size), rz

    rr = total([folded(r_ref[band] * r_ref[band]) for band in bands])
    vr = total([folded(v_ref[band] * r_ref[band]) for band in bands])
    shadow = drop * vr
    for band in bands:
        x_ref[band] = jnp.zeros_like(r_ref[band])
        direct(band, r_ref[band] - shadow * v_ref[band])
    lax.while_loop(open_still, body, (jnp.int32(0), jnp.float32(1.0), weighed(rr, vr)))


def solve_kernel(ridge, *refs):
    pieces = refs[:8]
    cross_ref, old_hbm, f_hbm, r_hbm, coef_ref, out_ref, pieces_ref, old_ref, upper, lower, f_ref, r_ref, x_ref, res_ref, p_ref, ap_ref, v_ref, parts_ref, delta_ref, sems = refs[8:]
    loads = [pltpu.make_async_copy(pieces[i], pieces_ref.at[i], sems.at[i]) for i in range(8)]
    rest = ((old_hbm, old_ref), (f_hbm, f_ref), (r_hbm, r_ref))
    loads += [pltpu.make_async_copy(there, here, sems.at[8 + i]) for i, (there, here) in enumerate(rest)]
    for load in loads:
        load.start()
    for shift in range(4):
        for other in range(2):
            loads[shift * 2 + other].wait()
            ref = pieces_ref.at[shift * 2 + other]
            px, pc = offsets(shift, other)
            row = pl.multiple_of(px * 128, 128)
            for group in range(3):
                for side in range(2):
                    lanes = pl.ds(pl.multiple_of(pc * 256 + side * 128, 128), 128)
                    block = ref[side * 16 : side * 16 + 16, group * 8 : group * 8 + 8, :].reshape(128, 128)
                    high, low = split_two(block)
                    upper[group, pl.ds(row, 128), lanes] = high
                    lower[group, pl.ds(row, 128), lanes] = low
    n = upper.shape[1]
    per = 32 // STEPS
    work = (x_ref, res_ref, p_ref, ap_ref, v_ref, parts_ref)
    loads[8].wait()
    res_ref[...] = cross_ref[:per].reshape(n, 128) - ridge * old_ref[0]
    conjugate_gradients(upper.at[0], lower.at[0], *work, ridge)
    first = x_ref[...]
    coef_ref[0] = old_ref[0] + first
    res_ref[...] = cross_ref[per:].reshape(n, 128) - ridge * old_ref[1] - times(upper[2], lower[2], first)
    high_first, low_first = split_two(first)
    delta_ref[:n, :128] = high_first
    delta_ref[:n, 128:] = low_first
    conjugate_gradients(upper.at[1], lower.at[1], *work, ridge)
    second = x_ref[...]
    coef_ref[1] = old_ref[1] + second
    high, low = split_two(second)
    delta_ref[n:, :128] = high
    delta_ref[n:, 128:] = low
    delta = delta_ref[...]
    tile = 256
    for load in loads[9:]:
        load.wait()
    for row in range(0, f_ref.shape[0], tile):
        both = jnp.dot(f_ref[row : row + tile, :], delta, preferred_element_type=F32)
        out_ref[row : row + tile, :] = r_ref[row : row + tile, :] - both[:, :128] - both[:, 128:]


def solve(pieces, cross, old, feats, residuals, ridge):
    def full(array):
        return pl.BlockSpec(array.shape, lambda: (0,) * array.ndim)

    return pl.pallas_call(
        functools.partial(solve_kernel, ridge),
        in_specs=[pl.BlockSpec(memory_space=pl.ANY)] * 8
        + [pl.BlockSpec(memory_space=pltpu.VMEM)]
        + [pl.BlockSpec(memory_space=pl.ANY)] * 3,
        out_specs=[full(old), full(residuals)],
        out_shape=[
            jax.ShapeDtypeStruct(old.shape, F32),
            jax.ShapeDtypeStruct(residuals.shape, F32),
        ],
        scratch_shapes=[
            pltpu.VMEM((8, 32, 24, 128), F32),
            pltpu.VMEM(old.shape, F32),
            pltpu.VMEM((3, 512, 512), BF),
            pltpu.VMEM((3, 512, 512), BF),
            pltpu.VMEM(feats.shape, BF),
            pltpu.VMEM(residuals.shape, F32),
            pltpu.VMEM((512, 128), F32),
            pltpu.VMEM((512, 128), F32),
            pltpu.VMEM((512, 128), F32),
            pltpu.VMEM((512, 128), F32),
            pltpu.VMEM((512, 128), F32),
            pltpu.VMEM((512, 256), BF),
            pltpu.VMEM((1024, 256), BF),
            pltpu.SemaphoreType.DMA((11,)),
        ],
        compiler_params=pltpu.CompilerParams(vmem_limit_bytes=51 << 20),
        name="solve",
    )(*pieces, cross, old, feats, residuals)


def copies_kernel(got_ref, gram_ref, cross_ref):
    summed = [got_ref[i] for i in range(got_ref.shape[0])]
    while len(summed) > 1:
        summed = [summed[i] + summed[i + 1] for i in range(0, len(summed), 2)]
    first = gram_ref.shape[1]
    gram_ref[...] = jnp.broadcast_to(summed[0][None, :first], gram_ref.shape)
    cross_ref[...] = jnp.broadcast_to(summed[0][None, first:], cross_ref.shape)


def copies_of_sum(got):
    whole = pl.BlockSpec(memory_space=pltpu.VMEM)
    return pl.pallas_call(
        copies_kernel,
        in_specs=[whole],
        out_specs=[whole, whole],
        out_shape=[
            jax.ShapeDtypeStruct((got.shape[0], 24, 128), F32),
            jax.ShapeDtypeStruct((got.shape[0], 32, 128), F32),
        ],
        name="copies",
    )(got)


def exchange(values, axes):
    return lax.all_to_all(values, axes, split_axis=0, concat_axis=0, tiled=True)


def spread(values):
    nx, nc = lax.axis_size("x"), lax.axis_size("c")
    moved = [values]
    for shift in range(1, nx):
        moved.append(lax.ppermute(values, "x", [(i, (i + shift) % nx) for i in range(nx)]))
    pieces = []
    for value in moved:
        pieces += [value, lax.ppermute(value, "c", [(i, (i + 1) % nc) for i in range(nc)])]
    return pieces


def body(embeddings, residuals, projections, phases, old_coef, block_order):
    local_blocks, _, width = projections.shape
    nrows = lax.axis_size("z") * lax.axis_size("y")
    ridge = 0.25 * (embeddings.shape[0] * nrows) / width

    got = exchange(payload(block_order, projections, phases, nrows), ROWS)
    copies, shifts = pick(block_order, got, local_blocks)
    weights = spread(exchange(copies, ROWS))
    feats, parts = features(weights, embeddings, shifts, residuals)

    gram_copies, cross_copies = copies_of_sum(exchange(parts, ROWS))
    grams = exchange(gram_copies, ROWS)
    cross_copies, grams = lax.optimization_barrier((cross_copies, grams))
    pieces = spread(grams)
    cross = exchange(cross_copies, ROWS)
    coef, current = solve(pieces, cross, old_coef, feats, residuals, ridge)
    return current, coef


def solution(mesh):
    grid = Mesh(mesh.devices.reshape(8, 4, 4, 2), ROWS + CLS)
    in_specs = (
        P(ROWS, None),
        P(ROWS, CLS),
        P(ROWS, None, None),
        P(ROWS, None),
        P(None, None, CLS),
        P(),
    )
    out_specs = (P(ROWS, CLS), P(None, None, CLS))
    return jax.shard_map(body, mesh=grid, in_specs=in_specs, out_specs=out_specs, check_vma=False)
```
